32 devices in a mesh: row: 8 (over z, y), col: 4 (over x, core).
Axes of the slice: x: 2, y: 2, z: 4, core: 2. Of those that a mesh axis runs over, the one named last changes fastest.
Arguments:
- contact_map: float32 [256, 256], P('row', 'col'), may hold values from -6 to 6
- embed_weight: bfloat16 [16, 128], replicated, may hold values from -1.5 to 1.5
- embed_bias: float32 [128], replicated, may hold values from -3 to 3
- conv_weight: bfloat16 [3, 3, 3, 128, 128], replicated, may hold values from -0.1875 to 0.1875
- conv_bias: float32 [3, 128], replicated, may hold values from -3 to 3
- mix_weight: bfloat16 [128, 128], replicated, may hold values from -0.5 to 0.5
- mix_bias: float32 [128], replicated, may hold values from -6 to 6
- proj_weight: bfloat16 [128, 256], replicated, may hold values from -1 to 1
- proj_bias: float32 [256], replicated, may hold values from -3 to 3
- up_weight: bfloat16 [256, 1024], replicated, may hold values from -0.375 to 0.375
- up_bias: float32 [1024], replicated, may hold values from -3 to 3
- down_weight: bfloat16 [1024, 256], replicated, may hold values from -0.1875 to 0.1875
- down_bias: float32 [256], replicated, may hold values from -3 to 3
Outputs:
- latents: bfloat16 [64, 256], P(('row', 'col'))
- sym: bfloat16 [64, 64, 128], P('row', 'col')
The draws below stay inside these ranges and needn't reach their ends.
All inputs are finite; a program needn't handle non-finite values.
Results may differ from the reference program's by a relative error of at most 0.0085.
Values may be sent and summed in bfloat16 or wider, within the bound.
No kernel may reach another device: no remote copies, remote signals or barrier semaphores. Data moves between devices by JAX's collectives and lax.ppermute only.
A program may use at most 64 MiB of HBM per device.

```python
import jax
import jax.numpy as jnp
from jax import lax

PATCH = 4
C = 128
L = 256
HID = 1024
LAYERS = 3
NP = 64
PIX = 256


def shard_levels(stream_key, dims, cuts, smallest, top_value):
    gain, own = 1.0, jax.random.fold_in(stream_key, 6)
    for axis_at, shards_of in cuts:
        steps = jnp.exp(jax.random.uniform(jax.random.fold_in(own, axis_at), (shards_of,), jnp.float32, smallest / len(cuts), top_value / len(cuts)))
        gain = gain * jnp.repeat(steps, dims[axis_at] // shards_of).reshape([-1 if axis == axis_at else 1 for axis in range(len(dims))])
    return gain


def centred(rng, shape, spread, bound, shards=(), kind=jnp.bfloat16):
    values = jax.random.normal(rng, shape, jnp.float32) * spread
    if len(shards) > 0:
        values = shard_levels(rng, shape, shards, -0.22, 0.18) * values
    return jnp.clip(values, min=-bound, max=bound).astype(kind)


def setup_inputs(seed: int = 0) -> dict:
    keys = jax.random.split(jax.random.key(seed), 14)
    return {
        "contact_map": centred(keys[0], (PIX, PIX), 1.0, 6.0, ((0, 8), (1, 4)), jnp.float32),
        "embed_weight": centred(keys[1], (PATCH * PATCH, C), (PATCH * PATCH) ** -0.5, 1.5),
        "embed_bias": centred(keys[2], (C,), 0.5, 3.0, (), jnp.float32),
        "conv_weight": centred(keys[3], (LAYERS, 3, 3, C, C), (9 * C) ** -0.5, 0.1875),
        "conv_bias": centred(keys[4], (LAYERS, C), 0.5, 3.0, (), jnp.float32),
        "mix_weight": centred(keys[5], (C, C), C ** -0.5, 0.5),
        "mix_bias": centred(keys[6], (C,), 1.0, 6.0, (), jnp.float32),
        "proj_weight": centred(keys[7], (C, L), (C // 4) ** -0.5, 1.0),
        "proj_bias": centred(keys[8], (L,), 0.5, 3.0, (), jnp.float32),
        "up_weight": centred(keys[9], (L, HID), L ** -0.5, 0.375),
        "up_bias": centred(keys[10], (HID,), 0.5, 3.0, (), jnp.float32),
        "down_weight": centred(keys[11], (HID, L), HID ** -0.5, 0.1875),
        "down_bias": centred(keys[12], (L,), 0.5, 3.0, (), jnp.float32),
    }


def reference(contact_map, embed_weight, embed_bias, conv_weight, conv_bias, mix_weight, mix_bias, proj_weight, proj_bias, up_weight, up_bias, down_weight, down_bias):
    grid = contact_map.reshape(NP, PATCH, NP, PATCH).transpose(0, 2, 1, 3)
    patches = grid.reshape(NP * NP, PATCH * PATCH).astype(jnp.bfloat16)
    feat = jnp.dot(patches, embed_weight, preferred_element_type=jnp.float32) + embed_bias
    feat = feat.astype(jnp.bfloat16).reshape(NP, NP, C)
    for layer in range(LAYERS):
        lhs = feat.astype(jnp.float32)[None]
        rhs = conv_weight[layer].astype(jnp.float32)
        out = lax.conv_general_dilated(lhs, rhs, (1, 1), "SAME", dimension_numbers=("NHWC", "HWIO", "NHWC"), precision=lax.Precision.HIGHEST)[0]
        feat = jax.nn.gelu(out + conv_bias[layer]).astype(jnp.bfloat16)
    whole = feat.astype(jnp.float32)
    sym = ((whole + whole.transpose(1, 0, 2)) * 0.5).astype(jnp.bfloat16)
    mixed = jax.nn.gelu(jnp.dot(sym.reshape(NP * NP, C), mix_weight, preferred_element_type=jnp.float32) + mix_bias)
    pooled = (jnp.sum(mixed.reshape(NP, NP, C), axis=1) / NP).astype(jnp.bfloat16)
    latent = jnp.dot(pooled, proj_weight, preferred_element_type=jnp.float32) + proj_bias
    hidden = jax.nn.gelu(jnp.dot(latent.astype(jnp.bfloat16), up_weight, preferred_element_type=jnp.float32) + up_bias).astype(jnp.bfloat16)
    result = latent + jnp.dot(hidden, down_weight, preferred_element_type=jnp.float32) + down_bias
    return result.astype(jnp.bfloat16), sym
```

```python
import functools

import jax
import jax.numpy as jnp
from jax import lax
from jax.experimental import pallas as pl
from jax.experimental.pallas import tpu as pltpu
from jax.sharding import PartitionSpec as P

PATCH = 4
LAYERS = 3
UNROLL_CELLS = 2048
CHUNK_CELLS = 256


def gelu(x):
    scale = 0.7978845608028654
    half = 0.5 * x
    return half + half * jnp.tanh(x * (scale + (scale * 0.044715) * (x * x)))


def for_rows(total, span, step):
    if total * span <= UNROLL_CELLS:
        chunk = max(1, CHUNK_CELLS // span)
        for start in range(0, total, chunk):
            step(start, min(chunk, total - start))
    else:
        lax.fori_loop(0, total, lambda r, carry: (step(r, 1), carry)[1], 0)


def encoder_kernel(
    gathered, embed_w, embed_b, conv_w, conv_b, mix_w, mix_b, proj_w, proj_b,
    up_w, up_b, down_w, down_b, latents, sym_out, *buffers, tile_rows, tile_cols, shared,
):
    n_row, n_col, pixels, cells = gathered.shape
    width = embed_w.shape[1]
    span = n_row * tile_rows
    own_rows = latents.shape[0]
    row = lax.axis_index("row")
    col = lax.axis_index("col")
    origin = row * tile_rows - LAYERS

    def keep_inside(value, first):
        rows = first + lax.broadcasted_iota(jnp.int32, value.shape, 0)
        return jnp.where((rows >= 0) & (rows < span), value, 0.0)

    def emit(target, start, value):
        count = value.shape[0]
        place = lax.broadcasted_iota(jnp.int32, value.shape, 1)
        left = jnp.where(place == 0, 0.0, pltpu.roll(value, 1, 1))
        right = jnp.where(place == span - 1, 0.0, pltpu.roll(value, span - 1, 1))
        for at, part in enumerate((left, value, right)):
            target[pl.ds(start, count), :, at * width : (at + 1) * width] = part.astype(jnp.bfloat16)

    def block_weight(group):
        tiled = jnp.concatenate([embed_w[...].astype(jnp.float32)] * group, axis=0)
        tiled = jnp.concatenate([tiled] * group, axis=1)
        at_row = lax.broadcasted_iota(jnp.int32, tiled.shape, 0) // pixels
        at_col = lax.broadcasted_iota(jnp.int32, tiled.shape, 1) // width
        return jnp.where(at_row == at_col, tiled, 0.0).astype(jnp.bfloat16)

    def embed(target, flipped):
        group, inner = (n_row, tile_rows) if flipped else (n_col, tile_cols)
        weight = block_weight(group)
        bias = embed_b[...].reshape(1, width)
        bias = jnp.concatenate([bias] * group, axis=1)
        if flipped:
            first_tile = (origin + tile_cols) // tile_cols - 1
            firsts = [r * tile_rows - LAYERS for r in range(n_row)]
            count = max(
                (f + tile_rows + 2 * LAYERS - 1) // tile_cols - f // tile_cols + 1 for f in firsts
            )
            tiles = [first_tile + t for t in range(count)]
            limit = n_col - 1
            outer = tile_cols
        else:
            tiles = [row - 1, row, row + 1]
            limit = n_row - 1
            outer = tile_rows

        def step(start, rows):
            shape = (rows, inner, cells)
            major = lax.broadcasted_iota(jnp.int32, shape, 0) + start + origin
            minor = lax.broadcasted_iota(jnp.int32, shape, 1)
            lane = lax.broadcasted_iota(jnp.int32, shape, 2)
            picked = None
            for tile in tiles:
                offset = major - tile * outer
                ok = (offset >= 0) & (offset < outer)
                goal = minor * tile_cols + offset if flipped else offset * tile_cols + minor
                select = jnp.where(ok & (lane == goal), 1.0, 0.0)
                select = select.reshape(rows * inner, cells).astype(jnp.bfloat16)
                at = jnp.clip(tile, 0, limit)
                source = gathered[:, at] if flipped else gathered[at]
                source = source.reshape(group * pixels, cells)
                part = lax.dot_general(
                    select, source, (((1,), (1,)), ((), ())), preferred_element_type=jnp.float32
                )
                picked = part if picked is None else picked + part
            value = jnp.dot(picked.astype(jnp.bfloat16), weight, preferred_element_type=jnp.float32)
            value = value + bias
            value = jnp.concatenate(
                [
                    value[:, g * width : (g + 1) * width].reshape(rows, inner, width)
                    for g in range(group)
                ],
                axis=1,
            )
            emit(target, start, keep_inside(value, start + origin))

        for_rows(tile_rows + 2 * LAYERS, span, step)

    def taps(layer, flipped):
        if flipped:
            return [conv_w[layer, :, a].reshape(3 * width, width) for a in range(3)]
        return [conv_w[layer, a].reshape(3 * width, width) for a in range(3)]

    def convolve(source, layer, flipped, start, rows, place, extent):
        total = conv_b[layer : layer + 1, :]
        for a, weight in enumerate(taps(layer, flipped)):
            window = source[pl.ds(start + a, rows), pl.ds(place, extent), :]
            window = window.reshape(rows * extent, 3 * width)
            total = total + jnp.dot(window, weight, preferred_element_type=jnp.float32)
        return gelu(total).reshape(rows, extent, width)

    def features(flipped, first, second, third):
        embed(first, flipped)
        for layer, source, target in ((0, first, second), (1, second, third)):

            def step(start, rows, layer=layer, source=source, target=target):
                value = convolve(source, layer, flipped, start, rows, 0, span)
                emit(target, start, keep_inside(value, start + origin + layer + 1))

            for_rows(tile_rows + 2 * (LAYERS - layer - 1), span, step)
        place = pl.multiple_of(col * tile_cols, tile_cols)
        tile = convolve(third, LAYERS - 1, flipped, 0, tile_rows, place, tile_cols)
        strip = convolve(third, LAYERS - 1, flipped, col * own_rows, own_rows, 0, span)
        return tile.astype(jnp.bfloat16), strip.astype(jnp.bfloat16)

    def average(first, second):
        total = first.astype(jnp.float32) + second.astype(jnp.float32)
        return (total * 0.5).astype(jnp.bfloat16)

    one, two, three = buffers[:3]
    tile, strip = features(False, one, two, three)
    if shared:
        four, five, six = one, two, three
    else:
        four, five, six = buffers[3:6]
    flipped_tile, flipped_strip = features(True, four, five, six)
    sym_out[...] = average(tile, flipped_tile)
    sym = average(strip, flipped_strip).reshape(own_rows * span, width)
    mixed = jnp.dot(sym, mix_w[...], preferred_element_type=jnp.float32) + mix_b[...].reshape(1, width)
    summed = jnp.sum(gelu(mixed).reshape(own_rows, span, width), axis=1)
    pooled = (summed / span).astype(jnp.bfloat16)
    latent = jnp.dot(pooled, proj_w[...], preferred_element_type=jnp.float32)
    latent = latent + proj_b[...].reshape(1, -1)
    hidden = jnp.dot(latent.astype(jnp.bfloat16), up_w[...], preferred_element_type=jnp.float32)
    hidden = gelu(hidden + up_b[...].reshape(1, -1)).astype(jnp.bfloat16)
    result = jnp.dot(hidden, down_w[...], preferred_element_type=jnp.float32)
    latents[...] = (latent + result + down_b[...].reshape(1, -1)).astype(jnp.bfloat16)


def body(contact_map, embed_weight, *rest):
    n_row, n_col = lax.axis_size("row"), lax.axis_size("col")
    tile_rows = contact_map.shape[0] // PATCH
    tile_cols = contact_map.shape[1] // PATCH
    pixels, width = embed_weight.shape
    cells = tile_rows * tile_cols
    grid = contact_map.astype(jnp.bfloat16).reshape(tile_rows, PATCH, tile_cols, PATCH)
    patches = grid.transpose(1, 3, 0, 2).reshape(1, pixels, cells)
    sent = jnp.broadcast_to(patches, (n_row * n_col, pixels, cells))
    gathered = lax.all_to_all(sent, ("row", "col"), 0, 0, tiled=True)
    gathered = gathered.reshape(n_row, n_col, pixels, cells)
    span = n_row * tile_rows
    own_rows = tile_rows // n_col
    out_width = rest[-1].shape[0]
    heights = [tile_rows + 2 * (LAYERS - layer) for layer in range(LAYERS)]
    buffers = [pltpu.VMEM((h, span, 3 * width), jnp.bfloat16) for h in heights]
    shared = sum(heights) * span > UNROLL_CELLS * 2
    if not shared:
        buffers = buffers * 2
    whole = pl.BlockSpec(memory_space=pltpu.VMEM)
    kernel = functools.partial(
        encoder_kernel, tile_rows=tile_rows, tile_cols=tile_cols, shared=shared
    )
    return pl.pallas_call(
        kernel,
        out_shape=(
            jax.ShapeDtypeStruct((own_rows, out_width), jnp.bfloat16),
            jax.ShapeDtypeStruct((tile_rows, tile_cols, width), jnp.bfloat16),
        ),
        in_specs=[whole] * (2 + len(rest)),
        out_specs=(whole, whole),
        scratch_shapes=buffers,
        name="encoder",
    )(gathered, embed_weight, *rest)


def solution(mesh):
    return jax.shard_map(
        body,
        mesh=mesh,
        in_specs=(P("row", "col"), P(), P(), P(), P(), P(), P(), P(), P(), P(), P(), P(), P()),
        out_specs=(P(("row", "col"), None), P("row", "col", None)),
        check_vma=False,
    )
```

```python
import functools
import itertools

import jax
import jax.numpy as jnp
from jax import lax
from jax.experimental import pallas as pl
from jax.experimental.pallas import tpu as pltpu
from jax.sharding import PartitionSpec as P

PATCH = 4
LAYERS = 3
UNROLL_CELLS = 2048
CHUNK_CELLS = 768
PAD = 8


def gelu(x):
    scale = 0.7978845608028654
    half = 0.5 * x
    return half + half * jnp.tanh(x * (scale + (scale * 0.044715) * (x * x)))


def row_steps(total, span, step):
    if total * span <= UNROLL_CELLS:
        chunk = max(1, CHUNK_CELLS // span)
        starts = range(0, total, chunk)
        return [functools.partial(step, s, min(chunk, total - s)) for s in starts]
    return [lambda: lax.fori_loop(0, total, lambda r, carry: (step(r, 1), carry)[1], 0)]


def in_turn(first, second):
    for mine, other in itertools.zip_longest(first, second):
        for thunk in (mine, other):
            if thunk is not None:
                thunk()


def encoder_kernel(
    gathered, embed_w, embed_b, conv_w, conv_b, mix_w, mix_b, proj_w, proj_b,
    up_w, up_b, down_w, down_b, latents, sym_out, *buffers, tile_rows, tile_cols, shared,
):
    remote = [embed_b, conv_w, mix_b, proj_b, up_b, down_w, down_b]
    arrived, local, buffers = buffers[0], buffers[1 : 1 + len(remote)], buffers[1 + len(remote) :]
    loads = [
        pltpu.make_async_copy(source, target, arrived.at[at])
        for at, (source, target) in enumerate(zip(remote, local))
    ]
    for load in loads:
        load.start()
    embed_b, conv_w, mix_b, proj_b, up_b, down_w, down_b = local
    n_row, n_col, pixels, cells = gathered.shape
    width = embed_w.shape[1]
    span = n_row * tile_rows
    own_rows = latents.shape[0]
    row = lax.axis_index("row")
    col = lax.axis_index("col")
    origin = row * tile_rows - LAYERS

    def keep_inside(value, first):
        rows = first + lax.broadcasted_iota(jnp.int32, value.shape, 0)
        return jnp.where((rows >= 0) & (rows < span), value, 0.0)

    def emit(pair, start, value):
        target, stage = pair
        count = value.shape[0]
        base = 0 if shared else start
        stage[pl.ds(base, count), PAD : PAD + span, :] = value
        for at in range(3):
            part = stage[pl.ds(base, count), PAD - 1 + at : PAD - 1 + at + span, :]
            target[pl.ds(start, count), :, at * width : (at + 1) * width] = part.astype(jnp.bfloat16)

    def block_weight(group):
        tiled = jnp.concatenate([embed_w[...].astype(jnp.float32)] * group, axis=0)
        tiled = jnp.concatenate([tiled] * group, axis=1)
        at_row = lax.broadcasted_iota(jnp.int32, tiled.shape, 0) // pixels
        at_col = lax.broadcasted_iota(jnp.int32, tiled.shape, 1) // width
        return jnp.where(at_row == at_col, tiled, 0.0).astype(jnp.bfloat16)

    def embed(target, flipped):
        group, inner = (n_row, tile_rows) if flipped else (n_col, tile_cols)
        weight = block_weight(group)
        bias = embed_b[...].reshape(1, width)
        bias = jnp.concatenate([bias] * group, axis=1)
        if flipped:
            first_tile = (origin + tile_cols) // tile_cols - 1
            firsts = [r * tile_rows - LAYERS for r in range(n_row)]
            count = max(
                (f + tile_rows + 2 * LAYERS - 1) // tile_cols - f // tile_cols + 1 for f in firsts
            )
            tiles = [first_tile + t for t in range(count)]
            limit = n_col - 1
            outer = tile_cols
        else:
            tiles = [row - 1, row, row + 1]
            limit = n_row - 1
            outer = tile_rows

        def step(start, rows):
            shape = (rows, inner, cells)
            major = lax.broadcasted_iota(jnp.int32, shape, 0) + start + origin
            minor = lax.broadcasted_iota(jnp.int32, shape, 1)
            lane = lax.broadcasted_iota(jnp.int32, shape, 2)
            picked = None
            for tile in tiles:
                offset = major - tile * outer
                ok = (offset >= 0) & (offset < outer)
                goal = minor * tile_cols + offset if flipped else offset * tile_cols + minor
                select = jnp.where(ok & (lane == goal), 1.0, 0.0)
                select = select.reshape(rows * inner, cells).astype(jnp.bfloat16)
                at = jnp.clip(tile, 0, limit)
                source = gathered[:, at] if flipped else gathered[at]
                source = source.reshape(group * pixels, cells)
                part = lax.dot_general(
                    select, source, (((1,), (1,)), ((), ())), preferred_element_type=jnp.float32
                )
                picked = part if picked is None else picked + part
            value = jnp.dot(picked.astype(jnp.bfloat16), weight, preferred_element_type=jnp.float32)
            value = value + bias
            value = jnp.concatenate(
                [
                    value[:, g * width : (g + 1) * width].reshape(rows, inner, width)
                    for g in range(group)
                ],
                axis=1,
            )
            emit(target, start, keep_inside(value, start + origin))

        return row_steps(tile_rows + 2 * LAYERS, span, step)

    def taps(layer, flipped):
        if flipped:
            return [conv_w[layer, :, a].reshape(3 * width, width) for a in range(3)]
        return [conv_w[layer, a].reshape(3 * width, width) for a in range(3)]

    def convolve(source, layer, flipped, start, rows, place, extent):
        windows = [
            source[pl.ds(start + a, rows), pl.ds(place, extent), :].reshape(rows * extent, 3 * width)
            for a in range(3)
        ]
        total = jnp.dot(
            jnp.concatenate(windows, axis=1),
            jnp.concatenate(taps(layer, flipped), axis=0),
            preferred_element_type=jnp.float32,
        )
        total = total + conv_b[layer : layer + 1, :]
        return gelu(total).reshape(rows, extent, width)

    def layer_steps(layer, flipped, source, target):
        def step(start, rows):
            value = convolve(source[0], layer, flipped, start, rows, 0, span)
            emit(target, start, keep_inside(value, start + origin + layer + 1))

        return row_steps(tile_rows + 2 * (LAYERS - layer - 1), span, step)

    def last_layer(flipped, source):
        place = pl.multiple_of(col * tile_cols, tile_cols)
        tile = convolve(source[0], LAYERS - 1, flipped, 0, tile_rows, place, tile_cols)
        strip = convolve(source[0], LAYERS - 1, flipped, col * own_rows, own_rows, 0, span)
        return tile.astype(jnp.bfloat16), strip.astype(jnp.bfloat16)

    def average(first, second):
        total = first.astype(jnp.float32) + second.astype(jnp.float32)
        return (total * 0.5).astype(jnp.bfloat16)

    half = len(buffers) // 2
    pairs = list(zip(buffers[:half], buffers[half:]))
    for _, stage in pairs:
        stage[:, :PAD, :] = jnp.zeros((stage.shape[0], PAD, width), jnp.float32)
        stage[:, PAD + span :, :] = jnp.zeros((stage.shape[0], PAD, width), jnp.float32)
    plain, turned = pairs[:LAYERS], pairs[-LAYERS:]
    loads[0].wait()
    if shared:
        for thunk in embed(plain[0], False):
            thunk()
        for load in loads[1:]:
            load.wait()
        for layer in range(LAYERS - 1):
            for thunk in layer_steps(layer, False, plain[layer], plain[layer + 1]):
                thunk()
        tile, strip = last_layer(False, plain[-1])
        for thunk in embed(turned[0], True):
            thunk()
        for layer in range(LAYERS - 1):
            for thunk in layer_steps(layer, True, turned[layer], turned[layer + 1]):
                thunk()
    else:
        in_turn(embed(plain[0], False), embed(turned[0], True))
        for load in loads[1:]:
            load.wait()
        for layer in range(LAYERS - 1):
            in_turn(
                layer_steps(layer, False, plain[layer], plain[layer + 1]),
                layer_steps(layer, True, turned[layer], turned[layer + 1]),
            )
        tile, strip = last_layer(False, plain[-1])
    flipped_tile, flipped_strip = last_layer(True, turned[-1])
    sym_out[...] = average(tile, flipped_tile)
    sym = average(strip, flipped_strip).reshape(own_rows * span, width)
    mixed = jnp.dot(sym, mix_w[...], preferred_element_type=jnp.float32) + mix_b[...].reshape(1, width)
    summed = jnp.sum(gelu(mixed).reshape(own_rows, span, width), axis=1)
    pooled = (summed / span).astype(jnp.bfloat16)
    latent = jnp.dot(pooled, proj_w[...], preferred_element_type=jnp.float32)
    latent = latent + proj_b[...].reshape(1, -1)
    hidden = jnp.dot(latent.astype(jnp.bfloat16), up_w[...], preferred_element_type=jnp.float32)
    hidden = gelu(hidden + up_b[...].reshape(1, -1)).astype(jnp.bfloat16)
    result = jnp.dot(hidden, down_w[...], preferred_element_type=jnp.float32)
    latents[...] = (latent + result + down_b[...].reshape(1, -1)).astype(jnp.bfloat16)


def body(contact_map, embed_weight, *rest):
    n_row, n_col = lax.axis_size("row"), lax.axis_size("col")
    tile_rows = contact_map.shape[0] // PATCH
    tile_cols = contact_map.shape[1] // PATCH
    pixels, width = embed_weight.shape
    cells = tile_rows * tile_cols
    grid = contact_map.astype(jnp.bfloat16).reshape(tile_rows, PATCH, tile_cols, PATCH)
    patches = grid.transpose(1, 3, 0, 2).reshape(1, pixels, cells)
    sent = jnp.broadcast_to(patches, (n_row * n_col, pixels, cells))
    gathered = lax.all_to_all(sent, ("row", "col"), 0, 0, tiled=True)
    gathered = gathered.reshape(n_row, n_col, pixels, cells)
    span = n_row * tile_rows
    own_rows = tile_rows // n_col
    out_width = rest[-1].shape[0]
    heights = [tile_rows + 2 * (LAYERS - layer) for layer in range(LAYERS)]
    buffers = [pltpu.VMEM((h, span, 3 * width), jnp.bfloat16) for h in heights]
    shared = sum(heights) * span > UNROLL_CELLS * 2
    stages = [
        pltpu.VMEM((1 if shared else h, span + 2 * PAD, width), jnp.float32) for h in heights
    ]
    if not shared:
        buffers, stages = buffers * 2, stages * 2
    whole = pl.BlockSpec(memory_space=pltpu.VMEM)
    operands = [gathered, embed_weight, *rest]
    in_specs = [whole] * len(operands)
    copied = []
    for at in (2, 3, 6, 8, 10, 11, 12):
        in_specs[at] = pl.BlockSpec(memory_space=pl.ANY)
        copied.append(pltpu.VMEM(operands[at].shape, operands[at].dtype))
    for at in range(len(operands)):
        if in_specs[at] is whole and (at > 0 or not shared):
            operands[at] = pltpu.with_memory_space_constraint(operands[at], pltpu.VMEM)
    kernel = functools.partial(
        encoder_kernel, tile_rows=tile_rows, tile_cols=tile_cols, shared=shared
    )
    return pl.pallas_call(
        kernel,
        out_shape=(
            jax.ShapeDtypeStruct((own_rows, out_width), jnp.bfloat16),
            jax.ShapeDtypeStruct((tile_rows, tile_cols, width), jnp.bfloat16),
        ),
        in_specs=in_specs,
        out_specs=(whole, whole),
        scratch_shapes=[pltpu.SemaphoreType.DMA((len(copied),))] + copied + buffers + stages,
        name="encoder",
    )(*operands)


def solution(mesh):
    return jax.shard_map(
        body,
        mesh=mesh,
        in_specs=(P("row", "col"), P(), P(), P(), P(), P(), P(), P(), P(), P(), P(), P(), P()),
        out_specs=(P(("row", "col"), None), P("row", "col", None)),
        check_vma=False,
    )
```

```python
import functools
import itertools

import jax
import jax.numpy as jnp
from jax import lax
from jax.experimental import pallas as pl
from jax.experimental.pallas import tpu as pltpu
from jax.sharding import PartitionSpec as P

PATCH = 4
LAYERS = 3
UNROLL_CELLS = 2048
CHUNK_CELLS = 768
PAD = 8
PIECE = 32
SLOT = 8


def gelu(x):
    scale = 0.7978845608028654
    half = 0.5 * x
    return half + half * jnp.tanh(x * (scale + (scale * 0.044715) * (x * x)))


def row_steps(total, span, step):
    if total * span <= UNROLL_CELLS:
        chunk = max(1, CHUNK_CELLS // span)
        starts = range(0, total, chunk)
        return [functools.partial(step, s, min(chunk, total - s)) for s in starts]
    return [lambda: lax.fori_loop(0, total, lambda r, carry: (step(r, 1), carry)[1], 0)]


def in_turn(first, second):
    for mine, other in itertools.zip_longest(first, second):
        for thunk in (mine, other):
            if thunk is not None:
                thunk()


def window_tiles(row, flipped, sizes):
    n_row, n_col, tile_rows, tile_cols = sizes
    if not flipped:
        return [row - 1, row, row + 1]
    first = (row * tile_rows - LAYERS + tile_cols) // tile_cols - 1
    starts = [r * tile_rows - LAYERS for r in range(n_row)]
    reach = tile_rows + 2 * LAYERS - 1
    count = max((f + reach) // tile_cols - f // tile_cols + 1 for f in starts)
    return [first + t for t in range(count)]


def selection(row, flipped, start, rows, sizes):
    n_row, n_col, tile_rows, tile_cols = sizes
    inner, outer, limit = (tile_rows, tile_cols, n_col) if flipped else (tile_cols, tile_rows, n_row)
    cells = tile_rows * tile_cols
    shape = (rows, inner, cells)
    major = lax.broadcasted_iota(jnp.int32, shape, 0) + (start + row * tile_rows - LAYERS)
    minor = lax.broadcasted_iota(jnp.int32, shape, 1)
    lane = lax.broadcasted_iota(jnp.int32, shape, 2)
    blocks = []
    for tile in window_tiles(row, flipped, sizes):
        offset = major - tile * outer
        goal = minor * tile_cols + offset if flipped else offset * tile_cols + minor
        ok = (offset >= 0) & (offset < outer) & (major >= 0) & (major < limit * outer)
        block = jnp.where(ok & (lane == goal), 1.0, 0.0)
        blocks.append(block.reshape(rows * inner, cells).astype(jnp.bfloat16))
    return jnp.concatenate(blocks, axis=1)


def split(value, count):
    parts = []
    for _ in range(count):
        part = value.astype(jnp.bfloat16).astype(jnp.float32)
        parts.append(part)
        value = value - part
    return parts


def patch_kernel(tile, sent, *, tile_rows, tile_cols):
    height, span = tile.shape
    cells = tile_rows * tile_cols
    shape = (span, PATCH * cells)
    pixel = lax.broadcasted_iota(jnp.int32, shape, 0)
    lane = lax.broadcasted_iota(jnp.int32, shape, 1)
    goal = (lane % tile_cols) * PATCH + lane // cells
    spread = jnp.where(pixel == goal, 1.0, 0.0).astype(jnp.bfloat16)
    wide = jnp.dot(tile[...].astype(jnp.bfloat16), spread, preferred_element_type=jnp.float32)
    line = lax.broadcasted_iota(jnp.int32, wide.shape, 0) // PATCH
    lane = lax.broadcasted_iota(jnp.int32, wide.shape, 1)
    wide = jnp.where(line == (lane % cells) // tile_cols, wide, 0.0)
    blocks = [wide[:, b * cells : (b + 1) * cells] for b in range(PATCH)]
    stacked = jnp.concatenate(blocks, axis=0).astype(jnp.bfloat16)
    shape = (PATCH * PATCH, PATCH * height)
    pixel = lax.broadcasted_iota(jnp.int32, shape, 0)
    lane = lax.broadcasted_iota(jnp.int32, shape, 1)
    mine = (lane % PATCH == pixel // PATCH) & (lane // height == pixel % PATCH)
    mine = jnp.where(mine, 1.0, 0.0).astype(jnp.bfloat16)
    result = jnp.dot(mine, stacked, preferred_element_type=jnp.float32).astype(jnp.bfloat16)
    sent[...] = jnp.broadcast_to(result[None], sent.shape)


def prepare_kernel(embed_w, embed_b, conv_w, *outs, sizes):
    pixels, width = embed_w.shape
    bias = jnp.concatenate(split(embed_b[...].reshape(1, width), 3), axis=0)
    rest = jnp.zeros((PIECE - pixels - 3, width), jnp.float32)
    left = jnp.concatenate([embed_w[...].astype(jnp.float32), bias, rest], axis=0)
    left = left.astype(jnp.bfloat16)
    products = {}
    for a, b in itertools.product(range(3), range(3)):
        products[a, b] = jnp.dot(left, conv_w[0, a, b], preferred_element_type=jnp.float32)
    for flipped, target in ((False, outs[0]), (True, outs[1])):
        for down in range(3):
            pieces, offsets = [], []
            for along in range(3):
                product = products[(along, down) if flipped else (down, along)]
                pieces += split(product[:pixels], 2)
                offset = jnp.sum(product[pixels : pixels + 3], axis=0, keepdims=True)
                offsets.append(jnp.concatenate(split(offset, 3), axis=0))
                offsets.append(jnp.zeros((SLOT - 3, width), jnp.float32))
            used = 3 * (2 * pixels + SLOT)
            offsets.append(jnp.zeros((width - used, width), jnp.float32))
            value = jnp.concatenate(pieces + offsets, axis=0)
            target[down * width : (down + 1) * width, :] = value.astype(jnp.bfloat16)
    if len(outs) > 2:
        row = lax.axis_index("row")
        for flipped, target in ((False, outs[2]), (True, outs[3])):
            target[...] = selection(row, flipped, 0, sizes[2] + 2 * LAYERS, sizes)


def encoder_kernel(
    gathered, first_plain, first_turned, conv_w, conv_b, mix_w, mix_b, proj_w, proj_b,
    up_w, up_b, down_w, down_b, *refs, sizes, shared,
):
    n_row, n_col, tile_rows, tile_cols = sizes
    if shared:
        selects = (None, None)
    else:
        selects, refs = refs[:2], refs[2:]
    latents, sym_out, refs = refs[0], refs[1], refs[2:]
    remote = [conv_w, mix_b, proj_b, up_b, down_w, down_b]
    arrived, local, buffers = refs[0], refs[1 : 1 + len(remote)], refs[1 + len(remote) :]
    loads = [
        pltpu.make_async_copy(source, target, arrived.at[at])
        for at, (source, target) in enumerate(zip(remote, local))
    ]
    for load in loads:
        load.start()
    conv_w, mix_b, proj_b, up_b, down_w, down_b = local
    _, pixels, cells = gathered.shape
    width = mix_w.shape[0]
    span = n_row * tile_rows
    own_rows = latents.shape[0]
    row = lax.axis_index("row")
    col = lax.axis_index("col")
    origin = row * tile_rows - LAYERS

    def keep_inside(value, first):
        rows = first + lax.broadcasted_iota(jnp.int32, value.shape, 0)
        return jnp.where((rows >= 0) & (rows < span), value, 0.0)

    def shifted(stage, start, value):
        count = value.shape[0]
        base = 0 if shared else start
        stage[pl.ds(base, count), PAD : PAD + span, :] = value
        return [
            stage[pl.ds(base, count), PAD - 1 + at : PAD - 1 + at + span, :] for at in range(3)
        ]

    def emit(pair, start, value):
        target, stage = pair
        for at, part in enumerate(shifted(stage, start, value)):
            lanes = slice(at * width, (at + 1) * width)
            target[pl.ds(start, value.shape[0]), :, lanes] = part.astype(jnp.bfloat16)

    def patches(pair, flipped):
        target, stage = pair
        group, inner = (n_row, tile_rows) if flipped else (n_col, tile_cols)
        limit = (n_col if flipped else n_row) - 1
        ones = jnp.ones((width - 6 * pixels, cells), jnp.bfloat16)
        columns = []
        for tile in window_tiles(row, flipped, sizes):
            at = jnp.clip(tile, 0, limit)
            stacked = []
            for g in range(group):
                source = gathered[g * n_col + at] if flipped else gathered[at * n_col + g]
                stacked += [source] * 6 + [ones]
            columns.append(jnp.concatenate(stacked, axis=0))
        source = jnp.concatenate(columns, axis=1)

        def step(start, rows):
            if shared:
                select = selection(row, flipped, start, rows, sizes)
            else:
                select = selects[flipped][start * inner : (start + rows) * inner, :]
            value = lax.dot_general(
                select, source, (((1,), (1,)), ((), ())), preferred_element_type=jnp.float32
            )
            value = jnp.concatenate(
                [
                    value[:, g * width : (g + 1) * width].reshape(rows, inner, width)
                    for g in range(group)
                ],
                axis=1,
            )
            before, same, after = shifted(stage, start, value)
            lane = lax.broadcasted_iota(jnp.int32, same.shape, 2)
            which = jnp.where(lane < 6 * pixels, lane // (2 * pixels), (lane - 6 * pixels) // SLOT)
            value = jnp.where(which == 0, before, jnp.where(which == 1, same, after))
            target[pl.ds(start, rows), :, :] = value.astype(jnp.bfloat16)

        return row_steps(tile_rows + 2 * LAYERS, span, step)

    def taps(layer, flipped):
        if layer == 0:
            return (first_turned if flipped else first_plain)[...]
        if flipped:
            blocks = [conv_w[layer, :, a].reshape(3 * width, width) for a in range(3)]
            return jnp.concatenate(blocks, axis=0)
        return conv_w[layer].reshape(9 * width, width)

    def convolve(source, layer, flipped, start, rows, place, extent):
        windows = [
            source[pl.ds(start + a, rows), pl.ds(place, extent), :].reshape(rows * extent, -1)
            for a in range(3)
        ]
        total = jnp.dot(
            jnp.concatenate(windows, axis=1),
            taps(layer, flipped),
            preferred_element_type=jnp.float32,
        )
        return gelu(total + conv_b[layer : layer + 1, :]).reshape(rows, extent, width)

    def layer_steps(layer, flipped, source, target):
        def step(start, rows):
            value = convolve(source[0], layer, flipped, start, rows, 0, span)
            emit(target, start, keep_inside(value, start + origin + layer + 1))

        return row_steps(tile_rows + 2 * (LAYERS - layer - 1), span, step)

    def last_strip(flipped, source):
        strip = convolve(source[0], LAYERS - 1, flipped, col * own_rows, own_rows, 0, span)
        return strip.astype(jnp.bfloat16)

    def last_tile(flipped, source):
        place = pl.multiple_of(col * tile_cols, tile_cols)
        tile = convolve(source[0], LAYERS - 1, flipped, 0, tile_rows, place, tile_cols)
        return tile.astype(jnp.bfloat16)

    def average(first, second):
        total = first.astype(jnp.float32) + second.astype(jnp.float32)
        return (total * 0.5).astype(jnp.bfloat16)

    half = len(buffers) // 2
    pairs = list(zip(buffers[:half], buffers[half:]))
    for _, stage in pairs:
        stage[:, :PAD, :] = jnp.zeros((stage.shape[0], PAD, width), jnp.float32)
        stage[:, PAD + span :, :] = jnp.zeros((stage.shape[0], PAD, width), jnp.float32)
    plain, turned = pairs[:LAYERS], pairs[-LAYERS:]
    if shared:
        for load in loads:
            load.wait()
        strips, tiles = [], []
        for flipped, chain in ((False, plain), (True, turned)):
            steps = patches(chain[0], flipped)
            for layer in range(LAYERS - 1):
                steps += layer_steps(layer, flipped, chain[layer], chain[layer + 1])
            for thunk in steps:
                thunk()
            strips.append(last_strip(flipped, chain[-1]))
            tiles.append(last_tile(flipped, chain[-1]))
    else:
        in_turn(patches(plain[0], False), patches(turned[0], True))
        in_turn(
            layer_steps(0, False, plain[0], plain[1]), layer_steps(0, True, turned[0], turned[1])
        )
        for load in loads:
            load.wait()
        for layer in range(1, LAYERS - 1):
            in_turn(
                layer_steps(layer, False, plain[layer], plain[layer + 1]),
                layer_steps(layer, True, turned[layer], turned[layer + 1]),
            )
        strips = [last_strip(False, plain[-1]), last_strip(True, turned[-1])]
        tiles = [last_tile(False, plain[-1]), last_tile(True, turned[-1])]
    sym_out[...] = average(*tiles)
    sym = average(*strips).reshape(own_rows * span, width)
    mixed = jnp.dot(sym, mix_w[...], preferred_element_type=jnp.float32) + mix_b[...].reshape(1, width)
    summed = jnp.sum(gelu(mixed).reshape(own_rows, span, width), axis=1)
    pooled = (summed / span).astype(jnp.bfloat16)
    latent = jnp.dot(pooled, proj_w[...], preferred_element_type=jnp.float32)
    latent = latent + proj_b[...].reshape(1, -1)
    hidden = jnp.dot(latent.astype(jnp.bfloat16), up_w[...], preferred_element_type=jnp.float32)
    hidden = gelu(hidden + up_b[...].reshape(1, -1)).astype(jnp.bfloat16)
    result = jnp.dot(hidden, down_w[...], preferred_element_type=jnp.float32)
    latents[...] = (latent + result + down_b[...].reshape(1, -1)).astype(jnp.bfloat16)


def body(contact_map, embed_weight, embed_bias, conv_weight, *rest):
    n_row, n_col = lax.axis_size("row"), lax.axis_size("col")
    tile_rows = contact_map.shape[0] // PATCH
    tile_cols = contact_map.shape[1] // PATCH
    sizes = (n_row, n_col, tile_rows, tile_cols)
    pixels, width = embed_weight.shape
    cells = tile_rows * tile_cols
    span = n_row * tile_rows
    own_rows = tile_rows // n_col
    out_width = rest[-1].shape[0]
    heights = [tile_rows + 2 * (LAYERS - layer) for layer in range(LAYERS)]
    shared = sum(heights) * span > UNROLL_CELLS * 2
    whole = pl.BlockSpec(memory_space=pltpu.VMEM)

    def near(value):
        return pltpu.with_memory_space_constraint(value, pltpu.VMEM)

    shape = (n_row * n_col, pixels, cells)
    sent = pl.pallas_call(
        functools.partial(patch_kernel, tile_rows=tile_rows, tile_cols=tile_cols),
        out_shape=(jax.ShapeDtypeStruct if shared else pltpu.VMEM)(shape, jnp.bfloat16),
        in_specs=[whole],
        out_specs=whole,
        name="patches",
    )(contact_map)
    gathered = lax.all_to_all(sent, ("row", "col"), 0, 0, tiled=True)
    shapes = [(3 * width, width)] * 2
    if not shared:
        turned_tiles = len(window_tiles(0, True, sizes))
        shapes.append((heights[0] * tile_cols, 3 * cells))
        shapes.append((heights[0] * tile_rows, turned_tiles * cells))
    prepared = pl.pallas_call(
        functools.partial(prepare_kernel, sizes=sizes),
        out_shape=[pltpu.VMEM(shape, jnp.bfloat16) for shape in shapes],
        in_specs=[whole] * 3,
        out_specs=[whole] * len(shapes),
        name="prepare",
    )(embed_weight, embed_bias, conv_weight)
    operands = [gathered, *prepared[:2], conv_weight, *rest, *prepared[2:]]
    in_specs = [whole] * len(operands)
    copied = []
    for at in (3, 6, 8, 10, 11, 12):
        in_specs[at] = pl.BlockSpec(memory_space=pl.ANY)
        copied.append(pltpu.VMEM(operands[at].shape, operands[at].dtype))
    for at in range(len(operands)):
        if in_specs[at] is whole and (2 < at < 13 or at == 0 and not shared):
            operands[at] = near(operands[at])
    buffers = [
        pltpu.VMEM((h, span, width * (3 if at else 1)), jnp.bfloat16) for at, h in enumerate(heights)
    ]
    stages = [
        pltpu.VMEM((1 if shared else h, span + 2 * PAD, width), jnp.float32) for h in heights
    ]
    if not shared:
        buffers, stages = buffers * 2, stages * 2
    return pl.pallas_call(
        functools.partial(encoder_kernel, sizes=sizes, shared=shared),
        out_shape=(
            jax.ShapeDtypeStruct((own_rows, out_width), jnp.bfloat16),
            jax.ShapeDtypeStruct((tile_rows, tile_cols, width), jnp.bfloat16),
        ),
        in_specs=in_specs,
        out_specs=(whole, whole),
        scratch_shapes=[pltpu.SemaphoreType.DMA((len(copied),))] + copied + buffers + stages,
        name="encoder",
    )(*operands)


def solution(mesh):
    return jax.shard_map(
        body,
        mesh=mesh,
        in_specs=(P("row", "col"), P(), P(), P(), P(), P(), P(), P(), P(), P(), P(), P(), P()),
        out_specs=(P(("row", "col"), None), P("row", "col", None)),
        check_vma=False,
    )
```

```python
import functools
import itertools

import jax
import jax.numpy as jnp
from jax import lax
from jax.experimental import pallas as pl
from jax.experimental.pallas import tpu as pltpu
from jax.sharding import PartitionSpec as P

PATCH = 4
LAYERS = 3
UNROLL_CELLS = 2048
CHUNK_CELLS = 768
PAD = 8
PIECE = 32
SLOT = 8


def gelu(x):
    scale = 0.7978845608028654
    half = 0.5 * x
    return half + half * jnp.tanh(x * (scale + (scale * 0.044715) * (x * x)))


def row_steps(total, span, step):
    if total * span <= UNROLL_CELLS:
        chunk = max(1, CHUNK_CELLS // span)
        starts = range(0, total, chunk)
        return [functools.partial(step, s, min(chunk, total - s)) for s in starts]
    return [lambda: lax.fori_loop(0, total, lambda r, carry: (step(r, 1), carry)[1], 0)]


def in_turn(first, second):
    for mine, other in itertools.zip_longest(first, second):
        for thunk in (mine, other):
            if thunk is not None:
                thunk()


def window_tiles(row, flipped, sizes):
    n_row, n_col, tile_rows, tile_cols = sizes
    if not flipped:
        return [row - 1, row, row + 1]
    first = (row * tile_rows - LAYERS + tile_cols) // tile_cols - 1
    starts = [r * tile_rows - LAYERS for r in range(n_row)]
    reach = tile_rows + 2 * LAYERS - 1
    count = max((f + reach) // tile_cols - f // tile_cols + 1 for f in starts)
    return [first + t for t in range(count)]


def selection(row, flipped, start, rows, sizes):
    n_row, n_col, tile_rows, tile_cols = sizes
    inner, outer, limit = (tile_rows, tile_cols, n_col) if flipped else (tile_cols, tile_rows, n_row)
    cells = tile_rows * tile_cols
    shape = (rows, inner, cells)
    major = lax.broadcasted_iota(jnp.int32, shape, 0) + (start + row * tile_rows - LAYERS)
    minor = lax.broadcasted_iota(jnp.int32, shape, 1)
    lane = lax.broadcasted_iota(jnp.int32, shape, 2)
    blocks = []
    for tile in window_tiles(row, flipped, sizes):
        offset = major - tile * outer
        goal = minor * tile_cols + offset if flipped else offset * tile_cols + minor
        ok = (offset >= 0) & (offset < outer) & (major >= 0) & (major < limit * outer)
        block = jnp.where(ok & (lane == goal), 1.0, 0.0)
        blocks.append(block.reshape(rows * inner, cells).astype(jnp.bfloat16))
    return jnp.concatenate(blocks, axis=1)


def split(value, count):
    parts = []
    for _ in range(count):
        part = value.astype(jnp.bfloat16).astype(jnp.float32)
        parts.append(part)
        value = value - part
    return parts


def patch_kernel(tile, sent, *, tile_rows, tile_cols):
    height, span = tile.shape
    cells = tile_rows * tile_cols
    shape = (span, PATCH * cells)
    pixel = lax.broadcasted_iota(jnp.int32, shape, 0)
    lane = lax.broadcasted_iota(jnp.int32, shape, 1)
    goal = (lane % tile_cols) * PATCH + lane // cells
    spread = jnp.where(pixel == goal, 1.0, 0.0).astype(jnp.bfloat16)
    wide = jnp.dot(tile[...].astype(jnp.bfloat16), spread, preferred_element_type=jnp.float32)
    line = lax.broadcasted_iota(jnp.int32, wide.shape, 0) // PATCH
    lane = lax.broadcasted_iota(jnp.int32, wide.shape, 1)
    wide = jnp.where(line == (lane % cells) // tile_cols, wide, 0.0)
    blocks = [wide[:, b * cells : (b + 1) * cells] for b in range(PATCH)]
    stacked = jnp.concatenate(blocks, axis=0).astype(jnp.bfloat16)
    shape = (PATCH * PATCH, PATCH * height)
    pixel = lax.broadcasted_iota(jnp.int32, shape, 0)
    lane = lax.broadcasted_iota(jnp.int32, shape, 1)
    mine = (lane % PATCH == pixel // PATCH) & (lane // height == pixel % PATCH)
    mine = jnp.where(mine, 1.0, 0.0).astype(jnp.bfloat16)
    result = jnp.dot(mine, stacked, preferred_element_type=jnp.float32).astype(jnp.bfloat16)
    sent[...] = jnp.broadcast_to(result[None], sent.shape)


def prepare_kernel(*refs, sizes, count, matrices):
    embed_w, embed_b, conv_w, *others = refs[:count]
    outs = refs[count : count + 2 + matrices]
    kept = refs[count + 2 + matrices : -4]
    embed_buf, bias_buf, conv_buf, arrived = refs[-4:]
    sources = [embed_w, embed_b, conv_w.at[0], conv_w.at[pl.ds(1, LAYERS - 1)], *others]
    targets = [embed_buf, bias_buf, conv_buf, *kept]
    loads = [
        pltpu.make_async_copy(source, target, arrived.at[at])
        for at, (source, target) in enumerate(zip(sources, targets))
    ]
    for load in loads:
        load.start()
    if matrices:
        row = lax.axis_index("row")
        for flipped, target in ((False, outs[2]), (True, outs[3])):
            target[...] = selection(row, flipped, 0, sizes[2] + 2 * LAYERS, sizes)
    for load in loads[:3]:
        load.wait()
    embed_w, embed_b = embed_buf, bias_buf
    pixels, width = embed_w.shape
    bias = jnp.concatenate(split(embed_b[...].reshape(1, width), 3), axis=0)
    rest = jnp.zeros((PIECE - pixels - 3, width), jnp.float32)
    left = jnp.concatenate([embed_w[...].astype(jnp.float32), bias, rest], axis=0)
    left = left.astype(jnp.bfloat16)
    products = {}
    for a, b in itertools.product(range(3), range(3)):
        products[a, b] = jnp.dot(left, conv_buf[a, b], preferred_element_type=jnp.float32)
    for flipped, target in ((False, outs[0]), (True, outs[1])):
        for down in range(3):
            pieces, offsets = [], []
            for along in range(3):
                product = products[(along, down) if flipped else (down, along)]
                pieces += split(product[:pixels], 2)
                offset = jnp.sum(product[pixels : pixels + 3], axis=0, keepdims=True)
                offsets.append(jnp.concatenate(split(offset, 3), axis=0))
                offsets.append(jnp.zeros((SLOT - 3, width), jnp.float32))
            used = 3 * (2 * pixels + SLOT)
            offsets.append(jnp.zeros((width - used, width), jnp.float32))
            value = jnp.concatenate(pieces + offsets, axis=0)
            target[down * width : (down + 1) * width, :] = value.astype(jnp.bfloat16)
    for load in loads[3:]:
        load.wait()


def encoder_kernel(
    gathered, first_plain, first_turned, *refs, sizes, shared,
):
    n_row, n_col, tile_rows, tile_cols = sizes
    if shared:
        selects = (None, None)
    else:
        selects, refs = refs[:2], refs[2:]
    conv_w, conv_b, mix_w, mix_b, proj_w, proj_b, up_w, up_b, down_w, down_b = refs[:10]
    latents, sym_out, *buffers = refs[10:]
    _, pixels, cells = gathered.shape
    width = mix_w.shape[0]
    span = n_row * tile_rows
    own_rows = latents.shape[0]
    row = lax.axis_index("row")
    col = lax.axis_index("col")
    origin = row * tile_rows - LAYERS

    def keep_inside(value, first):
        rows = first + lax.broadcasted_iota(jnp.int32, value.shape, 0)
        return jnp.where((rows >= 0) & (rows < span), value, 0.0)

    def shifted(stage, start, value):
        count = value.shape[0]
        base = 0 if shared else start
        stage[pl.ds(base, count), PAD : PAD + span, :] = value
        return [
            stage[pl.ds(base, count), PAD - 1 + at : PAD - 1 + at + span, :] for at in range(3)
        ]

    def emit(pair, start, value):
        target, stage = pair
        for at, part in enumerate(shifted(stage, start, value)):
            lanes = slice(at * width, (at + 1) * width)
            target[pl.ds(start, value.shape[0]), :, lanes] = part.astype(jnp.bfloat16)

    def patches(pair, flipped):
        target, stage = pair
        group, inner = (n_row, tile_rows) if flipped else (n_col, tile_cols)
        limit = (n_col if flipped else n_row) - 1
        ones = jnp.ones((width - 6 * pixels, cells), jnp.bfloat16)
        columns = []
        for tile in window_tiles(row, flipped, sizes):
            at = jnp.clip(tile, 0, limit)
            stacked = []
            for g in range(group):
                source = gathered[g * n_col + at] if flipped else gathered[at * n_col + g]
                stacked += [source] * 6 + [ones]
            columns.append(jnp.concatenate(stacked, axis=0))
        source = jnp.concatenate(columns, axis=1)

        def step(start, rows):
            if shared:
                select = selection(row, flipped, start, rows, sizes)
            else:
                select = selects[flipped][start * inner : (start + rows) * inner, :]
            value = lax.dot_general(
                select, source, (((1,), (1,)), ((), ())), preferred_element_type=jnp.float32
            )
            value = jnp.concatenate(
                [
                    value[:, g * width : (g + 1) * width].reshape(rows, inner, width)
                    for g in range(group)
                ],
                axis=1,
            )
            before, same, after = shifted(stage, start, value)
            lane = lax.broadcasted_iota(jnp.int32, same.shape, 2)
            which = jnp.where(lane < 6 * pixels, lane // (2 * pixels), (lane - 6 * pixels) // SLOT)
            value = jnp.where(which == 0, before, jnp.where(which == 1, same, after))
            target[pl.ds(start, rows), :, :] = value.astype(jnp.bfloat16)

        return row_steps(tile_rows + 2 * LAYERS, span, step)

    def taps(layer, flipped):
        if layer == 0:
            return (first_turned if flipped else first_plain)[...]
        if flipped:
            blocks = [conv_w[layer - 1, :, a].reshape(3 * width, width) for a in range(3)]
            return jnp.concatenate(blocks, axis=0)
        return conv_w[layer - 1].reshape(9 * width, width)

    def convolve(source, layer, flipped, start, rows, place, extent):
        windows = [
            source[pl.ds(start + a, rows), pl.ds(place, extent), :].reshape(rows * extent, -1)
            for a in range(3)
        ]
        total = jnp.dot(
            jnp.concatenate(windows, axis=1),
            taps(layer, flipped),
            preferred_element_type=jnp.float32,
        )
        return gelu(total + conv_b[layer : layer + 1, :]).reshape(rows, extent, width)

    def layer_steps(layer, flipped, source, target):
        def step(start, rows):
            value = convolve(source[0], layer, flipped, start, rows, 0, span)
            emit(target, start, keep_inside(value, start + origin + layer + 1))

        return row_steps(tile_rows + 2 * (LAYERS - layer - 1), span, step)

    def last_strip(flipped, source):
        strip = convolve(source[0], LAYERS - 1, flipped, col * own_rows, own_rows, 0, span)
        return strip.astype(jnp.bfloat16)

    def last_tile(flipped, source):
        place = pl.multiple_of(col * tile_cols, tile_cols)
        tile = convolve(source[0], LAYERS - 1, flipped, 0, tile_rows, place, tile_cols)
        return tile.astype(jnp.bfloat16)

    def average(first, second):
        total = first.astype(jnp.float32) + second.astype(jnp.float32)
        return (total * 0.5).astype(jnp.bfloat16)

    half = len(buffers) // 2
    pairs = list(zip(buffers[:half], buffers[half:]))
    for _, stage in pairs:
        stage[:, :PAD, :] = jnp.zeros((stage.shape[0], PAD, width), jnp.float32)
        stage[:, PAD + span :, :] = jnp.zeros((stage.shape[0], PAD, width), jnp.float32)
    plain, turned = pairs[:LAYERS], pairs[-LAYERS:]
    if shared:
        strips, tiles = [], []
        for flipped, chain in ((False, plain), (True, turned)):
            steps = patches(chain[0], flipped)
            for layer in range(LAYERS - 1):
                steps += layer_steps(layer, flipped, chain[layer], chain[layer + 1])
            for thunk in steps:
                thunk()
            strips.append(last_strip(flipped, chain[-1]))
            tiles.append(last_tile(flipped, chain[-1]))
    else:
        in_turn(patches(plain[0], False), patches(turned[0], True))
        in_turn(
            layer_steps(0, False, plain[0], plain[1]), layer_steps(0, True, turned[0], turned[1])
        )
        for layer in range(1, LAYERS - 1):
            in_turn(
                layer_steps(layer, False, plain[layer], plain[layer + 1]),
                layer_steps(layer, True, turned[layer], turned[layer + 1]),
            )
        strips = [last_strip(False, plain[-1]), last_strip(True, turned[-1])]
        tiles = [last_tile(False, plain[-1]), last_tile(True, turned[-1])]
    sym_out[...] = average(*tiles)
    sym = average(*strips).reshape(own_rows * span, width)
    mixed = jnp.dot(sym, mix_w[...], preferred_element_type=jnp.float32) + mix_b[...].reshape(1, width)
    summed = jnp.sum(gelu(mixed).reshape(own_rows, span, width), axis=1)
    pooled = (summed / span).astype(jnp.bfloat16)
    latent = jnp.dot(pooled, proj_w[...], preferred_element_type=jnp.float32)
    latent = latent + proj_b[...].reshape(1, -1)
    hidden = jnp.dot(latent.astype(jnp.bfloat16), up_w[...], preferred_element_type=jnp.float32)
    hidden = gelu(hidden + up_b[...].reshape(1, -1)).astype(jnp.bfloat16)
    result = jnp.dot(hidden, down_w[...], preferred_element_type=jnp.float32)
    latents[...] = (latent + result + down_b[...].reshape(1, -1)).astype(jnp.bfloat16)


def body(contact_map, embed_weight, embed_bias, conv_weight, *rest):
    n_row, n_col = lax.axis_size("row"), lax.axis_size("col")
    tile_rows = contact_map.shape[0] // PATCH
    tile_cols = contact_map.shape[1] // PATCH
    sizes = (n_row, n_col, tile_rows, tile_cols)
    pixels, width = embed_weight.shape
    cells = tile_rows * tile_cols
    span = n_row * tile_rows
    own_rows = tile_rows // n_col
    out_width = rest[-1].shape[0]
    heights = [tile_rows + 2 * (LAYERS - layer) for layer in range(LAYERS)]
    shared = sum(heights) * span > UNROLL_CELLS * 2
    whole = pl.BlockSpec(memory_space=pltpu.VMEM)

    def near(value):
        return pltpu.with_memory_space_constraint(value, pltpu.VMEM)

    shape = (n_row * n_col, pixels, cells)
    sent = pl.pallas_call(
        functools.partial(patch_kernel, tile_rows=tile_rows, tile_cols=tile_cols),
        out_shape=(jax.ShapeDtypeStruct if shared else pltpu.VMEM)(shape, jnp.bfloat16),
        in_specs=[whole],
        out_specs=whole,
        name="patches",
    )(contact_map)
    gathered = lax.all_to_all(sent, ("row", "col"), 0, 0, tiled=True)
    shapes = [(3 * width, width)] * 2
    if not shared:
        turned_tiles = len(window_tiles(0, True, sizes))
        shapes.append((heights[0] * tile_cols, 3 * cells))
        shapes.append((heights[0] * tile_rows, turned_tiles * cells))
    shapes = [pltpu.VMEM(shape, jnp.bfloat16) for shape in shapes]
    matrices = len(shapes) - 2
    later = (LAYERS - 1,) + conv_weight.shape[1:]
    shapes.append(pltpu.VMEM(later, conv_weight.dtype))
    shapes += [pltpu.VMEM(value.shape, value.dtype) for value in rest]
    inputs = (embed_weight, embed_bias, conv_weight, *rest)
    prepared = pl.pallas_call(
        functools.partial(prepare_kernel, sizes=sizes, count=len(inputs), matrices=matrices),
        out_shape=shapes,
        in_specs=[pl.BlockSpec(memory_space=pl.ANY)] * len(inputs),
        out_specs=[whole] * len(shapes),
        scratch_shapes=[
            pltpu.VMEM(embed_weight.shape, embed_weight.dtype),
            pltpu.VMEM(embed_bias.shape, embed_bias.dtype),
            pltpu.VMEM(conv_weight.shape[1:], conv_weight.dtype),
            pltpu.SemaphoreType.DMA((len(inputs) + 1,)),
        ],
        name="prepare",
    )(*inputs)
    prepared = [near(value) for value in prepared]
    operands = [gathered if shared else near(gathered), *prepared]
    in_specs = [whole] * len(operands)
    buffers = [
        pltpu.VMEM((h, span, width * (3 if at else 1)), jnp.bfloat16) for at, h in enumerate(heights)
    ]
    stages = [
        pltpu.VMEM((1 if shared else h, span + 2 * PAD, width), jnp.float32) for h in heights
    ]
    if not shared:
        buffers, stages = buffers * 2, stages * 2
    return pl.pallas_call(
        functools.partial(encoder_kernel, sizes=sizes, shared=shared),
        out_shape=(
            jax.ShapeDtypeStruct((own_rows, out_width), jnp.bfloat16),
            jax.ShapeDtypeStruct((tile_rows, tile_cols, width), jnp.bfloat16),
        ),
        in_specs=in_specs,
        out_specs=(whole, whole),
        scratch_shapes=buffers + stages,
        name="encoder",
    )(*operands)


def solution(mesh):
    return jax.shard_map(
        body,
        mesh=mesh,
        in_specs=(P("row", "col"), P(), P(), P(), P(), P(), P(), P(), P(), P(), P(), P(), P()),
        out_specs=(P(("row", "col"), None), P("row", "col", None)),
        check_vma=False,
    )
```

```python
import functools
import itertools

import jax
import jax.numpy as jnp
from jax import lax
from jax.experimental import pallas as pl
from jax.experimental.pallas import tpu as pltpu
from jax.sharding import PartitionSpec as P

PATCH = 4
LAYERS = 3
UNROLL_CELLS = 2048
CHUNK_CELLS = 768
PAD = 8
PIECE = 32
SLOT = 8
HALVED = (0, 1, 2, 3, 6, 7)


def gelu_of_twice(half):
    scale = 2 * 0.7978845608028654
    return half + half * jnp.tanh(half * (scale + (4 * scale * 0.044715) * (half * half)))


def row_steps(total, span, step):
    if total * span <= UNROLL_CELLS:
        chunk = max(1, CHUNK_CELLS // span)
        starts = range(0, total, chunk)
        return [functools.partial(step, s, min(chunk, total - s)) for s in starts]
    return [lambda: lax.fori_loop(0, total, lambda r, carry: (step(r, 1), carry)[1], 0)]


def in_turn(first, second):
    for mine, other in itertools.zip_longest(first, second):
        for thunk in (mine, other):
            if thunk is not None:
                thunk()


def window_tiles(row, flipped, sizes):
    n_row, n_col, tile_rows, tile_cols = sizes
    if not flipped:
        return [row - 1, row, row + 1]
    first = (row * tile_rows - LAYERS + tile_cols) // tile_cols - 1
    starts = [r * tile_rows - LAYERS for r in range(n_row)]
    reach = tile_rows + 2 * LAYERS - 1
    count = max((f + reach) // tile_cols - f // tile_cols + 1 for f in starts)
    return [first + t for t in range(count)]


def selection(row, flipped, start, rows, sizes):
    n_row, n_col, tile_rows, tile_cols = sizes
    inner, outer, limit = (tile_rows, tile_cols, n_col) if flipped else (tile_cols, tile_rows, n_row)
    cells = tile_rows * tile_cols
    shape = (rows, inner, cells)
    major = lax.broadcasted_iota(jnp.int32, shape, 0) + (start + row * tile_rows - LAYERS)
    minor = lax.broadcasted_iota(jnp.int32, shape, 1)
    lane = lax.broadcasted_iota(jnp.int32, shape, 2)
    blocks = []
    for tile in window_tiles(row, flipped, sizes):
        offset = major - tile * outer
        goal = minor * tile_cols + offset if flipped else offset * tile_cols + minor
        ok = (offset >= 0) & (offset < outer) & (major >= 0) & (major < limit * outer)
        block = jnp.where(ok & (lane == goal), 1.0, 0.0)
        blocks.append(block.reshape(rows * inner, cells).astype(jnp.bfloat16))
    return jnp.concatenate(blocks, axis=1)


def split(value, count):
    parts = []
    for _ in range(count):
        part = value.astype(jnp.bfloat16).astype(jnp.float32)
        parts.append(part)
        value = value - part
    return parts


def patch_kernel(tile, sent, *, tile_rows, tile_cols):
    height, span = tile.shape
    cells = tile_rows * tile_cols
    shape = (span, PATCH * cells)
    pixel = lax.broadcasted_iota(jnp.int32, shape, 0)
    lane = lax.broadcasted_iota(jnp.int32, shape, 1)
    goal = (lane % tile_cols) * PATCH + lane // cells
    spread = jnp.where(pixel == goal, 1.0, 0.0).astype(jnp.bfloat16)
    wide = jnp.dot(tile[...].astype(jnp.bfloat16), spread, preferred_element_type=jnp.float32)
    line = lax.broadcasted_iota(jnp.int32, wide.shape, 0) // PATCH
    lane = lax.broadcasted_iota(jnp.int32, wide.shape, 1)
    wide = jnp.where(line == (lane % cells) // tile_cols, wide, 0.0)
    blocks = [wide[:, b * cells : (b + 1) * cells] for b in range(PATCH)]
    stacked = jnp.concatenate(blocks, axis=0).astype(jnp.bfloat16)
    shape = (PATCH * PATCH, PATCH * height)
    pixel = lax.broadcasted_iota(jnp.int32, shape, 0)
    lane = lax.broadcasted_iota(jnp.int32, shape, 1)
    mine = (lane % PATCH == pixel // PATCH) & (lane // height == pixel % PATCH)
    mine = jnp.where(mine, 1.0, 0.0).astype(jnp.bfloat16)
    result = jnp.dot(mine, stacked, preferred_element_type=jnp.float32).astype(jnp.bfloat16)
    sent[...] = jnp.broadcast_to(result[None], sent.shape)


def prepare_kernel(*refs, sizes, count, matrices):
    embed_w, embed_b, conv_w, *others = refs[:count]
    outs = refs[count : count + 2 + matrices]
    kept = refs[count + 2 + matrices : -4]
    embed_buf, bias_buf, conv_buf, arrived = refs[-4:]
    sources = [embed_w, embed_b, conv_w.at[0], conv_w.at[pl.ds(1, LAYERS - 1)], *others]
    targets = [embed_buf, bias_buf, conv_buf, *kept]
    loads = [
        pltpu.make_async_copy(source, target, arrived.at[at])
        for at, (source, target) in enumerate(zip(sources, targets))
    ]
    for load in loads:
        load.start()
    if matrices:
        row = lax.axis_index("row")
        for flipped, target in ((False, outs[2]), (True, outs[3])):
            target[...] = selection(row, flipped, 0, sizes[2] + 2 * LAYERS, sizes)
    for load in loads[:3]:
        load.wait()
    embed_w, embed_b = embed_buf, bias_buf
    pixels, width = embed_w.shape
    bias = jnp.concatenate(split(embed_b[...].reshape(1, width), 3), axis=0)
    rest = jnp.zeros((PIECE - pixels - 3, width), jnp.float32)
    left = jnp.concatenate([embed_w[...].astype(jnp.float32), bias, rest], axis=0)
    left = (0.5 * left).astype(jnp.bfloat16)
    products = {}
    for a, b in itertools.product(range(3), range(3)):
        products[a, b] = jnp.dot(left, conv_buf[a, b], preferred_element_type=jnp.float32)
    for flipped, target in ((False, outs[0]), (True, outs[1])):
        for down in range(3):
            pieces, offsets = [], []
            for along in range(3):
                product = products[(along, down) if flipped else (down, along)]
                pieces += split(product[:pixels], 2)
                offset = jnp.sum(product[pixels : pixels + 3], axis=0, keepdims=True)
                offsets.append(jnp.concatenate(split(offset, 3), axis=0))
                offsets.append(jnp.zeros((SLOT - 3, width), jnp.float32))
            used = 3 * (2 * pixels + SLOT)
            offsets.append(jnp.zeros((width - used, width), jnp.float32))
            value = jnp.concatenate(pieces + offsets, axis=0)
            target[down * width : (down + 1) * width, :] = value.astype(jnp.bfloat16)
    for load in loads[3:]:
        load.wait()
    for at in HALVED:
        kept[at][...] = (0.5 * kept[at][...].astype(jnp.float32)).astype(kept[at].dtype)


def encoder_kernel(
    gathered, first_plain, first_turned, *refs, sizes, shared,
):
    n_row, n_col, tile_rows, tile_cols = sizes
    if shared:
        selects = (None, None)
    else:
        selects, refs = refs[:2], refs[2:]
    conv_w, conv_b, mix_w, mix_b, proj_w, proj_b, up_w, up_b, down_w, down_b = refs[:10]
    latents, sym_out, *buffers = refs[10:]
    _, pixels, cells = gathered.shape
    width = mix_w.shape[0]
    span = n_row * tile_rows
    own_rows = latents.shape[0]
    row = lax.axis_index("row")
    col = lax.axis_index("col")

    def keep_inside(value, start, margin):
        rows = value.shape[0]
        if isinstance(start, int):
            edges = [max(0, min(rows, edge - start)) for edge in (margin, margin + tile_rows)]
        else:
            edges = [rows, rows]
        pieces = []
        for low, high in ((0, edges[0]), (edges[1], rows)):
            first = row * tile_rows - margin + start + low
            lines = [
                jnp.where((first + r >= 0) & (first + r < span), value[low + r], 0.0)[None]
                for r in range(high - low)
            ]
            pieces.append(lines)
        inner = [value[edges[0] : edges[1]]] if edges[1] > edges[0] else []
        return jnp.concatenate(pieces[0] + inner + pieces[1], axis=0)

    def shifted(stage, start, value):
        count = value.shape[0]
        base = 0 if shared else start
        stage[pl.ds(base, count), PAD : PAD + span, :] = value
        return [
            stage[pl.ds(base, count), PAD - 1 + at : PAD - 1 + at + span, :] for at in range(3)
        ]

    def emit(pair, start, value):
        target, stage = pair
        for at, part in enumerate(shifted(stage, start, value)):
            lanes = slice(at * width, (at + 1) * width)
            target[pl.ds(start, value.shape[0]), :, lanes] = part.astype(jnp.bfloat16)

    def patches(pair, flipped):
        target, stage = pair
        group, inner = (n_row, tile_rows) if flipped else (n_col, tile_cols)
        limit = (n_col if flipped else n_row) - 1
        ones = jnp.ones((width - 6 * pixels, cells), jnp.bfloat16)
        columns = []
        for tile in window_tiles(row, flipped, sizes):
            at = jnp.clip(tile, 0, limit)
            stacked = []
            for g in range(group):
                source = gathered[g * n_col + at] if flipped else gathered[at * n_col + g]
                stacked += [source] * 6 + [ones]
            columns.append(jnp.concatenate(stacked, axis=0))
        source = jnp.concatenate(columns, axis=1)

        def step(start, rows):
            if shared:
                select = selection(row, flipped, start, rows, sizes)
            else:
                select = selects[flipped][start * inner : (start + rows) * inner, :]
            value = lax.dot_general(
                select, source, (((1,), (1,)), ((), ())), preferred_element_type=jnp.float32
            )
            value = jnp.concatenate(
                [
                    value[:, g * width : (g + 1) * width].reshape(rows, inner, width)
                    for g in range(group)
                ],
                axis=1,
            )
            before, same, after = shifted(stage, start, value)
            lane = lax.broadcasted_iota(jnp.int32, same.shape, 2)
            which = jnp.where(lane < 6 * pixels, lane // (2 * pixels), (lane - 6 * pixels) // SLOT)
            value = jnp.where(which == 0, before, jnp.where(which == 1, same, after))
            target[pl.ds(start, rows), :, :] = value.astype(jnp.bfloat16)

        return row_steps(tile_rows + 2 * LAYERS, span, step)

    def taps(layer, flipped):
        if layer == 0:
            return (first_turned if flipped else first_plain)[...]
        if flipped:
            blocks = [conv_w[layer - 1, :, a].reshape(3 * width, width) for a in range(3)]
            return jnp.concatenate(blocks, axis=0)
        return conv_w[layer - 1].reshape(9 * width, width)

    def convolve(source, layer, flipped, start, rows, place, extent):
        windows = [
            source[pl.ds(start + a, rows), pl.ds(place, extent), :].reshape(rows * extent, -1)
            for a in range(3)
        ]
        total = jnp.dot(
            jnp.concatenate(windows, axis=1),
            taps(layer, flipped),
            preferred_element_type=jnp.float32,
        )
        return gelu_of_twice(total + conv_b[layer : layer + 1, :]).reshape(rows, extent, width)

    def layer_steps(layer, flipped, source, target):
        def step(start, rows):
            value = convolve(source[0], layer, flipped, start, rows, 0, span)
            emit(target, start, keep_inside(value, start, LAYERS - layer - 1))

        return row_steps(tile_rows + 2 * (LAYERS - layer - 1), span, step)

    def last_layer(flipped, source):
        place = pl.multiple_of(col * tile_cols, tile_cols)
        windows = [
            jnp.concatenate(
                [
                    source[0][pl.ds(col * own_rows + a, own_rows), :, :].reshape(own_rows * span, -1),
                    source[0][a : a + tile_rows, pl.ds(place, tile_cols), :].reshape(cells, -1),
                ],
                axis=0,
            )
            for a in range(3)
        ]
        total = jnp.dot(
            jnp.concatenate(windows, axis=1),
            taps(LAYERS - 1, flipped),
            preferred_element_type=jnp.float32,
        )
        total = gelu_of_twice(total + conv_b[LAYERS - 1 :, :]).astype(jnp.bfloat16)
        strip = total[: own_rows * span].reshape(own_rows, span, width)
        return strip, total[own_rows * span :].reshape(tile_rows, tile_cols, width)

    def average(first, second):
        total = first.astype(jnp.float32) + second.astype(jnp.float32)
        return (total * 0.5).astype(jnp.bfloat16)

    half = len(buffers) // 2
    pairs = list(zip(buffers[:half], buffers[half:]))
    for _, stage in pairs:
        stage[:, :PAD, :] = jnp.zeros((stage.shape[0], PAD, width), jnp.float32)
        stage[:, PAD + span :, :] = jnp.zeros((stage.shape[0], PAD, width), jnp.float32)
    plain, turned = pairs[:LAYERS], pairs[-LAYERS:]
    if shared:
        strips, tiles = [], []
        for flipped, chain in ((False, plain), (True, turned)):
            steps = patches(chain[0], flipped)
            for layer in range(LAYERS - 1):
                steps += layer_steps(layer, flipped, chain[layer], chain[layer + 1])
            for thunk in steps:
                thunk()
            strip, tile = last_layer(flipped, chain[-1])
            strips.append(strip)
            tiles.append(tile)
    else:
        in_turn(patches(plain[0], False), patches(turned[0], True))
        in_turn(
            layer_steps(0, False, plain[0], plain[1]), layer_steps(0, True, turned[0], turned[1])
        )
        for layer in range(1, LAYERS - 1):
            in_turn(
                layer_steps(layer, False, plain[layer], plain[layer + 1]),
                layer_steps(layer, True, turned[layer], turned[layer + 1]),
            )
        strips, tiles = zip(last_layer(False, plain[-1]), last_layer(True, turned[-1]))
    sym_out[...] = average(*tiles)
    sym = average(*strips).reshape(own_rows * span, width)
    mixed = jnp.dot(sym, mix_w[...], preferred_element_type=jnp.float32) + mix_b[...].reshape(1, width)
    summed = jnp.sum(gelu_of_twice(mixed).reshape(own_rows, span, width), axis=1)
    pooled = (summed / span).astype(jnp.bfloat16)
    latent = jnp.dot(pooled, proj_w[...], preferred_element_type=jnp.float32)
    latent = latent + proj_b[...].reshape(1, -1)
    hidden = jnp.dot(latent.astype(jnp.bfloat16), up_w[...], preferred_element_type=jnp.float32)
    hidden = gelu_of_twice(hidden + up_b[...].reshape(1, -1)).astype(jnp.bfloat16)
    result = jnp.dot(hidden, down_w[...], preferred_element_type=jnp.float32)
    latents[...] = (latent + result + down_b[...].reshape(1, -1)).astype(jnp.bfloat16)


def body(contact_map, embed_weight, embed_bias, conv_weight, *rest):
    n_row, n_col = lax.axis_size("row"), lax.axis_size("col")
    tile_rows = contact_map.shape[0] // PATCH
    tile_cols = contact_map.shape[1] // PATCH
    sizes = (n_row, n_col, tile_rows, tile_cols)
    pixels, width = embed_weight.shape
    cells = tile_rows * tile_cols
    span = n_row * tile_rows
    own_rows = tile_rows // n_col
    out_width = rest[-1].shape[0]
    heights = [tile_rows + 2 * (LAYERS - layer) for layer in range(LAYERS)]
    shared = sum(heights) * span > UNROLL_CELLS * 2
    whole = pl.BlockSpec(memory_space=pltpu.VMEM)

    def near(value):
        return pltpu.with_memory_space_constraint(value, pltpu.VMEM)

    shape = (n_row * n_col, pixels, cells)
    sent = pl.pallas_call(
        functools.partial(patch_kernel, tile_rows=tile_rows, tile_cols=tile_cols),
        out_shape=(jax.ShapeDtypeStruct if shared else pltpu.VMEM)(shape, jnp.bfloat16),
        in_specs=[whole],
        out_specs=whole,
        name="patches",
    )(contact_map)
    gathered = lax.all_to_all(sent, ("row", "col"), 0, 0, tiled=True)
    shapes = [(3 * width, width)] * 2
    if not shared:
        turned_tiles = len(window_tiles(0, True, sizes))
        shapes.append((heights[0] * tile_cols, 3 * cells))
        shapes.append((heights[0] * tile_rows, turned_tiles * cells))
    shapes = [pltpu.VMEM(shape, jnp.bfloat16) for shape in shapes]
    matrices = len(shapes) - 2
    later = (LAYERS - 1,) + conv_weight.shape[1:]
    shapes.append(pltpu.VMEM(later, conv_weight.dtype))
    shapes += [pltpu.VMEM(value.shape, value.dtype) for value in rest]
    inputs = (embed_weight, embed_bias, conv_weight, *rest)
    prepared = pl.pallas_call(
        functools.partial(prepare_kernel, sizes=sizes, count=len(inputs), matrices=matrices),
        out_shape=shapes,
        in_specs=[pl.BlockSpec(memory_space=pl.ANY)] * len(inputs),
        out_specs=[whole] * len(shapes),
        scratch_shapes=[
            pltpu.VMEM(embed_weight.shape, embed_weight.dtype),
            pltpu.VMEM(embed_bias.shape, embed_bias.dtype),
            pltpu.VMEM(conv_weight.shape[1:], conv_weight.dtype),
            pltpu.SemaphoreType.DMA((len(inputs) + 1,)),
        ],
        name="prepare",
    )(*inputs)
    prepared = [near(value) for value in prepared]
    operands = [gathered if shared else near(gathered), *prepared]
    in_specs = [whole] * len(operands)
    buffers = [
        pltpu.VMEM((h, span, width * (3 if at else 1)), jnp.bfloat16) for at, h in enumerate(heights)
    ]
    stages = [
        pltpu.VMEM((1 if shared else h, span + 2 * PAD, width), jnp.float32) for h in heights
    ]
    if not shared:
        buffers, stages = buffers * 2, stages * 2
    return pl.pallas_call(
        functools.partial(encoder_kernel, sizes=sizes, shared=shared),
        out_shape=(
            jax.ShapeDtypeStruct((own_rows, out_width), jnp.bfloat16),
            jax.ShapeDtypeStruct((tile_rows, tile_cols, width), jnp.bfloat16),
        ),
        in_specs=in_specs,
        out_specs=(whole, whole),
        scratch_shapes=buffers + stages,
        name="encoder",
    )(*operands)


def solution(mesh):
    return jax.shard_map(
        body,
        mesh=mesh,
        in_specs=(P("row", "col"), P(), P(), P(), P(), P(), P(), P(), P(), P(), P(), P(), P()),
        out_specs=(P(("row", "col"), None), P("row", "col", None)),
        check_vma=False,
    )
```

```python
import functools
import itertools

import jax
import jax.numpy as jnp
from jax import lax
from jax.experimental import pallas as pl
from jax.experimental.pallas import tpu as pltpu
from jax.sharding import PartitionSpec as P

PATCH = 4
LAYERS = 3
UNROLL_CELLS = 2048
CHUNK_CELLS = 768
PAD = 8
PIECE = 32
SLOT = 8


def gelu_of_twice(half):
    scale = 2 * 0.7978845608028654
    return half + half * jnp.tanh(half * (scale + (4 * scale * 0.044715) * (half * half)))


def row_steps(total, span, step):
    if total * span <= UNROLL_CELLS:
        chunk = max(1, CHUNK_CELLS // span)
        starts = range(0, total, chunk)
        return [functools.partial(step, s, min(chunk, total - s)) for s in starts]
    return [lambda: lax.fori_loop(0, total, lambda r, carry: (step(r, 1), carry)[1], 0)]


def in_turn(first, second):
    for mine, other in itertools.zip_longest(first, second):
        for thunk in (mine, other):
            if thunk is not None:
                thunk()


def window_tiles(row, flipped, sizes):
    n_row, n_col, tile_rows, tile_cols = sizes
    if not flipped:
        return [row - 1, row, row + 1]
    first = (row * tile_rows - LAYERS + tile_cols) // tile_cols - 1
    starts = [r * tile_rows - LAYERS for r in range(n_row)]
    reach = tile_rows + 2 * LAYERS - 1
    count = max((f + reach) // tile_cols - f // tile_cols + 1 for f in starts)
    return [first + t for t in range(count)]


def selection(row, flipped, start, rows, sizes):
    n_row, n_col, tile_rows, tile_cols = sizes
    inner, outer, limit = (tile_rows, tile_cols, n_col) if flipped else (tile_cols, tile_rows, n_row)
    cells = tile_rows * tile_cols
    shape = (rows, inner, cells)
    major = lax.broadcasted_iota(jnp.int32, shape, 0) + (start + row * tile_rows - LAYERS)
    minor = lax.broadcasted_iota(jnp.int32, shape, 1)
    lane = lax.broadcasted_iota(jnp.int32, shape, 2)
    blocks = []
    for tile in window_tiles(row, flipped, sizes):
        offset = major - tile * outer
        goal = minor * tile_cols + offset if flipped else offset * tile_cols + minor
        ok = (offset >= 0) & (offset < outer) & (major >= 0) & (major < limit * outer)
        block = jnp.where(ok & (lane == goal), 1.0, 0.0)
        blocks.append(block.reshape(rows * inner, cells).astype(jnp.bfloat16))
    return jnp.concatenate(blocks, axis=1)


def split(value, count):
    parts = []
    for _ in range(count):
        part = value.astype(jnp.bfloat16).astype(jnp.float32)
        parts.append(part)
        value = value - part
    return parts


def patch_kernel(tile, sent, *, tile_rows, tile_cols):
    height, span = tile.shape
    cells = tile_rows * tile_cols
    shape = (span, PATCH * cells)
    pixel = lax.broadcasted_iota(jnp.int32, shape, 0)
    lane = lax.broadcasted_iota(jnp.int32, shape, 1)
    goal = (lane % tile_cols) * PATCH + lane // cells
    spread = jnp.where(pixel == goal, 1.0, 0.0).astype(jnp.bfloat16)
    wide = jnp.dot(tile[...].astype(jnp.bfloat16), spread, preferred_element_type=jnp.float32)
    line = lax.broadcasted_iota(jnp.int32, wide.shape, 0) // PATCH
    lane = lax.broadcasted_iota(jnp.int32, wide.shape, 1)
    wide = jnp.where(line == (lane % cells) // tile_cols, wide, 0.0)
    blocks = [wide[:, b * cells : (b + 1) * cells] for b in range(PATCH)]
    stacked = jnp.concatenate(blocks, axis=0).astype(jnp.bfloat16)
    shape = (PATCH * PATCH, PATCH * height)
    pixel = lax.broadcasted_iota(jnp.int32, shape, 0)
    lane = lax.broadcasted_iota(jnp.int32, shape, 1)
    mine = (lane % PATCH == pixel // PATCH) & (lane // height == pixel % PATCH)
    mine = jnp.where(mine, 1.0, 0.0).astype(jnp.bfloat16)
    result = jnp.dot(mine, stacked, preferred_element_type=jnp.float32).astype(jnp.bfloat16)
    sent[...] = jnp.broadcast_to(result[None], sent.shape)


def prepare_kernel(*refs, sizes, count, matrices):
    embed_w, embed_b, conv_w, *others = refs[:count]
    outs = refs[count : count + 2 + matrices]
    kept = refs[count + 2 + matrices : -6]
    conv_w_kept, conv_b, mix_w, mix_b, proj_w, proj_b, up_w, up_b, _, _ = kept
    embed_buf, bias_buf, conv_buf, mix_buf, up_buf, arrived = refs[-6:]
    sources = [embed_w, embed_b, conv_w.at[0], conv_w.at[pl.ds(1, LAYERS - 1)], *others]
    targets = [embed_buf, bias_buf, conv_buf, *kept]
    targets[5], targets[9] = mix_buf, up_buf
    loads = [
        pltpu.make_async_copy(source, target, arrived.at[at])
        for at, (source, target) in enumerate(zip(sources, targets))
    ]
    for load in loads:
        load.start()
    if matrices:
        row = lax.axis_index("row")
        for flipped, target in ((False, outs[2]), (True, outs[3])):
            target[...] = selection(row, flipped, 0, sizes[2] + 2 * LAYERS, sizes)
    for load in loads[:3]:
        load.wait()
    embed_w, embed_b = embed_buf, bias_buf
    pixels, width = embed_w.shape
    bias = jnp.concatenate(split(embed_b[...].reshape(1, width), 3), axis=0)
    rest = jnp.zeros((PIECE - pixels - 3, width), jnp.float32)
    left = jnp.concatenate([embed_w[...].astype(jnp.float32), bias, rest], axis=0)
    left = (0.5 * left).astype(jnp.bfloat16)
    products = {}
    for a, b in itertools.product(range(3), range(3)):
        products[a, b] = jnp.dot(left, conv_buf[a, b], preferred_element_type=jnp.float32)
    for flipped, target in ((False, outs[0]), (True, outs[1])):
        for down in range(3):
            pieces, offsets = [], []
            for along in range(3):
                product = products[(along, down) if flipped else (down, along)]
                pieces += split(product[:pixels], 2)
                offset = jnp.sum(product[pixels : pixels + 3], axis=0, keepdims=True)
                offsets.append(jnp.concatenate(split(offset, 3), axis=0))
                offsets.append(jnp.zeros((SLOT - 3, width), jnp.float32))
            used = 3 * (2 * pixels + SLOT)
            offsets.append(jnp.zeros((width - used, width), jnp.float32))
            value = jnp.concatenate(pieces + offsets, axis=0)
            target[down * width : (down + 1) * width, :] = value.astype(jnp.bfloat16)
    for load in loads[3:]:
        load.wait()
    for ref in (conv_w_kept, conv_b, mix_b):
        ref[...] = (0.5 * ref[...].astype(jnp.float32)).astype(ref.dtype)
    quarter = (0.25 * mix_buf[...].astype(jnp.float32)).astype(jnp.bfloat16)
    mix_w[...] = jnp.concatenate([quarter, quarter], axis=0)
    half = (0.5 * up_buf[...].astype(jnp.float32)).astype(jnp.bfloat16)
    joint = jnp.dot(proj_w[...], half, preferred_element_type=jnp.float32)
    up_w[...] = jnp.concatenate(split(joint, 2), axis=0).astype(jnp.bfloat16)
    pieces = jnp.concatenate(split(proj_b[...].reshape(1, -1), 3), axis=0).astype(jnp.bfloat16)
    shift = jnp.dot(pieces, half, preferred_element_type=jnp.float32)
    up_b[...] = 0.5 * up_b[...] + jnp.sum(shift, axis=0)


def encoder_kernel(
    gathered, first_plain, first_turned, *refs, sizes, shared,
):
    n_row, n_col, tile_rows, tile_cols = sizes
    if shared:
        selects = (None, None)
    else:
        selects, refs = refs[:2], refs[2:]
    conv_w, conv_b, mix_w, mix_b, proj_w, proj_b, up_w, up_b, down_w, down_b = refs[:10]
    latents, sym_out, *buffers = refs[10:]
    _, pixels, cells = gathered.shape
    width = mix_w.shape[1]
    span = n_row * tile_rows
    own_rows = latents.shape[0]
    row = lax.axis_index("row")
    col = lax.axis_index("col")

    def keep_inside(value, start, margin):
        rows = value.shape[0]
        if isinstance(start, int):
            edges = [max(0, min(rows, edge - start)) for edge in (margin, margin + tile_rows)]
        else:
            edges = [rows, rows]
        pieces = []
        for low, high in ((0, edges[0]), (edges[1], rows)):
            first = row * tile_rows - margin + start + low
            lines = [
                jnp.where((first + r >= 0) & (first + r < span), value[low + r], 0.0)[None]
                for r in range(high - low)
            ]
            pieces.append(lines)
        inner = [value[edges[0] : edges[1]]] if edges[1] > edges[0] else []
        return jnp.concatenate(pieces[0] + inner + pieces[1], axis=0)

    def shifted(stage, start, value):
        count = value.shape[0]
        base = 0 if shared else start
        stage[pl.ds(base, count), PAD : PAD + span, :] = value
        return [
            stage[pl.ds(base, count), PAD - 1 + at : PAD - 1 + at + span, :] for at in range(3)
        ]

    def emit(pair, start, value):
        target, stage = pair
        for at, part in enumerate(shifted(stage, start, value)):
            lanes = slice(at * width, (at + 1) * width)
            target[pl.ds(start, value.shape[0]), :, lanes] = part.astype(jnp.bfloat16)

    def patches(pair, flipped):
        target, stage = pair
        group, inner = (n_row, tile_rows) if flipped else (n_col, tile_cols)
        limit = (n_col if flipped else n_row) - 1
        ones = jnp.ones((width - 6 * pixels, cells), jnp.bfloat16)
        columns = []
        for tile in window_tiles(row, flipped, sizes):
            at = jnp.clip(tile, 0, limit)
            stacked = []
            for g in range(group):
                source = gathered[at * n_row + g] if flipped else gathered[g * n_row + at]
                stacked += [source] * 6 + [ones]
            columns.append(jnp.concatenate(stacked, axis=0))
        source = jnp.concatenate(columns, axis=1)

        def step(start, rows):
            if shared:
                select = selection(row, flipped, start, rows, sizes)
            else:
                select = selects[flipped][start * inner : (start + rows) * inner, :]
            value = lax.dot_general(
                select, source, (((1,), (1,)), ((), ())), preferred_element_type=jnp.float32
            )
            value = jnp.concatenate(
                [
                    value[:, g * width : (g + 1) * width].reshape(rows, inner, width)
                    for g in range(group)
                ],
                axis=1,
            )
            before, same, after = shifted(stage, start, value)
            lane = lax.broadcasted_iota(jnp.int32, same.shape, 2)
            which = jnp.where(lane < 6 * pixels, lane // (2 * pixels), (lane - 6 * pixels) // SLOT)
            value = jnp.where(which == 0, before, jnp.where(which == 1, same, after))
            target[pl.ds(start, rows), :, :] = value.astype(jnp.bfloat16)

        return row_steps(tile_rows + 2 * LAYERS, span, step)

    def taps(layer, flipped):
        if layer == 0:
            return (first_turned if flipped else first_plain)[...]
        if flipped:
            blocks = [conv_w[layer - 1, :, a].reshape(3 * width, width) for a in range(3)]
            return jnp.concatenate(blocks, axis=0)
        return conv_w[layer - 1].reshape(9 * width, width)

    def convolve(source, layer, flipped, start, rows, place, extent):
        windows = [
            source[pl.ds(start + a, rows), pl.ds(place, extent), :].reshape(rows * extent, -1)
            for a in range(3)
        ]
        total = jnp.dot(
            jnp.concatenate(windows, axis=1),
            taps(layer, flipped),
            preferred_element_type=jnp.float32,
        )
        return gelu_of_twice(total + conv_b[layer : layer + 1, :]).reshape(rows, extent, width)

    def layer_steps(layer, flipped, source, target):
        def step(start, rows):
            value = convolve(source[0], layer, flipped, start, rows, 0, span)
            emit(target, start, keep_inside(value, start, LAYERS - layer - 1))

        return row_steps(tile_rows + 2 * (LAYERS - layer - 1), span, step)

    def last_layer(flipped, source):
        place = pl.multiple_of(col * tile_cols, tile_cols)
        windows = [
            jnp.concatenate(
                [
                    source[0][pl.ds(col * own_rows + a, own_rows), :, :].reshape(own_rows * span, -1),
                    source[0][a : a + tile_rows, pl.ds(place, tile_cols), :].reshape(cells, -1),
                ],
                axis=0,
            )
            for a in range(3)
        ]
        total = jnp.dot(
            jnp.concatenate(windows, axis=1),
            taps(LAYERS - 1, flipped),
            preferred_element_type=jnp.float32,
        )
        total = gelu_of_twice(total + conv_b[LAYERS - 1 :, :]).astype(jnp.bfloat16)
        strip = total[: own_rows * span].reshape(own_rows, span, width)
        return strip, total[own_rows * span :].reshape(tile_rows, tile_cols, width)

    def average(first, second):
        total = first.astype(jnp.float32) + second.astype(jnp.float32)
        return (total * 0.5).astype(jnp.bfloat16)

    half = len(buffers) // 2
    pairs = list(zip(buffers[:half], buffers[half:]))
    for _, stage in pairs:
        stage[:, :PAD, :] = jnp.zeros((stage.shape[0], PAD, width), jnp.float32)
        stage[:, PAD + span :, :] = jnp.zeros((stage.shape[0], PAD, width), jnp.float32)
    plain, turned = pairs[:LAYERS], pairs[-LAYERS:]
    if shared:
        strips, tiles = [], []
        for flipped, chain in ((False, plain), (True, turned)):
            steps = patches(chain[0], flipped)
            for layer in range(LAYERS - 1):
                steps += layer_steps(layer, flipped, chain[layer], chain[layer + 1])
            for thunk in steps:
                thunk()
            strip, tile = last_layer(flipped, chain[-1])
            strips.append(strip)
            tiles.append(tile)
    else:
        in_turn(patches(plain[0], False), patches(turned[0], True))
        in_turn(
            layer_steps(0, False, plain[0], plain[1]), layer_steps(0, True, turned[0], turned[1])
        )
        for layer in range(1, LAYERS - 1):
            in_turn(
                layer_steps(layer, False, plain[layer], plain[layer + 1]),
                layer_steps(layer, True, turned[layer], turned[layer + 1]),
            )
        strips, tiles = zip(last_layer(False, plain[-1]), last_layer(True, turned[-1]))
    sym_out[...] = average(*tiles)
    both = jnp.concatenate([s.reshape(own_rows * span, width) for s in strips], axis=1)
    mixed = jnp.dot(both, mix_w[...], preferred_element_type=jnp.float32) + mix_b[...].reshape(1, width)
    summed = jnp.sum(gelu_of_twice(mixed).reshape(own_rows, span, width), axis=1)
    pooled = (summed / span).astype(jnp.bfloat16)
    latent = jnp.dot(pooled, proj_w[...], preferred_element_type=jnp.float32)
    latent = latent + proj_b[...].reshape(1, -1)
    twice = jnp.concatenate([pooled, pooled], axis=1)
    hidden = jnp.dot(twice, up_w[...], preferred_element_type=jnp.float32)
    hidden = gelu_of_twice(hidden + up_b[...].reshape(1, -1)).astype(jnp.bfloat16)
    result = jnp.dot(hidden, down_w[...], preferred_element_type=jnp.float32)
    latents[...] = (latent + result + down_b[...].reshape(1, -1)).astype(jnp.bfloat16)


def body(contact_map, embed_weight, embed_bias, conv_weight, *rest):
    n_row, n_col = lax.axis_size("row"), lax.axis_size("col")
    tile_rows = contact_map.shape[0] // PATCH
    tile_cols = contact_map.shape[1] // PATCH
    sizes = (n_row, n_col, tile_rows, tile_cols)
    pixels, width = embed_weight.shape
    cells = tile_rows * tile_cols
    span = n_row * tile_rows
    own_rows = tile_rows // n_col
    out_width = rest[-1].shape[0]
    heights = [tile_rows + 2 * (LAYERS - layer) for layer in range(LAYERS)]
    shared = sum(heights) * span > UNROLL_CELLS * 2
    whole = pl.BlockSpec(memory_space=pltpu.VMEM)

    def near(value):
        return pltpu.with_memory_space_constraint(value, pltpu.VMEM)

    shape = (n_row * n_col, pixels, cells)
    sent = pl.pallas_call(
        functools.partial(patch_kernel, tile_rows=tile_rows, tile_cols=tile_cols),
        out_shape=(jax.ShapeDtypeStruct if shared else pltpu.VMEM)(shape, jnp.bfloat16),
        in_specs=[whole],
        out_specs=whole,
        name="patches",
    )(contact_map)
    gathered = lax.all_to_all(sent, ("col", "row"), 0, 0, tiled=True)
    shapes = [(3 * width, width)] * 2
    if not shared:
        turned_tiles = len(window_tiles(0, True, sizes))
        shapes.append((heights[0] * tile_cols, 3 * cells))
        shapes.append((heights[0] * tile_rows, turned_tiles * cells))
    shapes = [pltpu.VMEM(shape, jnp.bfloat16) for shape in shapes]
    matrices = len(shapes) - 2
    later = (LAYERS - 1,) + conv_weight.shape[1:]
    shapes.append(pltpu.VMEM(later, conv_weight.dtype))
    shapes += [pltpu.VMEM(value.shape, value.dtype) for value in rest]
    mix_weight, up_weight = rest[1], rest[5]
    shapes[matrices + 4] = pltpu.VMEM((2 * width, width), jnp.bfloat16)
    shapes[matrices + 8] = pltpu.VMEM((2 * width, up_weight.shape[1]), jnp.bfloat16)
    inputs = (embed_weight, embed_bias, conv_weight, *rest)
    prepared = pl.pallas_call(
        functools.partial(prepare_kernel, sizes=sizes, count=len(inputs), matrices=matrices),
        out_shape=shapes,
        in_specs=[pl.BlockSpec(memory_space=pl.ANY)] * len(inputs),
        out_specs=[whole] * len(shapes),
        scratch_shapes=[
            pltpu.VMEM(embed_weight.shape, embed_weight.dtype),
            pltpu.VMEM(embed_bias.shape, embed_bias.dtype),
            pltpu.VMEM(conv_weight.shape[1:], conv_weight.dtype),
            pltpu.VMEM(mix_weight.shape, mix_weight.dtype),
            pltpu.VMEM(up_weight.shape, up_weight.dtype),
            pltpu.SemaphoreType.DMA((len(inputs) + 1,)),
        ],
        name="prepare",
    )(*inputs)
    prepared = [near(value) for value in prepared]
    operands = [gathered if shared else near(gathered), *prepared]
    in_specs = [whole] * len(operands)
    buffers = [
        pltpu.VMEM((h, span, width * (3 if at else 1)), jnp.bfloat16) for at, h in enumerate(heights)
    ]
    stages = [
        pltpu.VMEM((1 if shared else h, span + 2 * PAD, width), jnp.float32) for h in heights
    ]
    if not shared:
        buffers, stages = buffers * 2, stages * 2
    return pl.pallas_call(
        functools.partial(encoder_kernel, sizes=sizes, shared=shared),
        out_shape=(
            jax.ShapeDtypeStruct((own_rows, out_width), jnp.bfloat16),
            jax.ShapeDtypeStruct((tile_rows, tile_cols, width), jnp.bfloat16),
        ),
        in_specs=in_specs,
        out_specs=(whole, whole),
        scratch_shapes=buffers + stages,
        name="encoder",
    )(*operands)


def solution(mesh):
    return jax.shard_map(
        body,
        mesh=mesh,
        in_specs=(P("row", "col"), P(), P(), P(), P(), P(), P(), P(), P(), P(), P(), P(), P()),
        out_specs=(P(("row", "col"), None), P("row", "col", None)),
        check_vma=False,
    )
```

```python
import functools
import itertools

import jax
import jax.numpy as jnp
from jax import lax
from jax.experimental import pallas as pl
from jax.experimental.pallas import tpu as pltpu
from jax.sharding import PartitionSpec as P

PATCH = 4
LAYERS = 3
UNROLL_CELLS = 2048
CHUNK_CELLS = 1024
PAD = 8
PIECE = 32
SLOT = 8


def gelu_of_twice(half):
    scale = 2 * 0.7978845608028654
    return half + half * jnp.tanh(half * (scale + (4 * scale * 0.044715) * (half * half)))


def row_steps(total, span, step):
    if total * span <= UNROLL_CELLS:
        chunk = max(1, CHUNK_CELLS // span)
        starts = range(0, total, chunk)
        return [functools.partial(step, s, min(chunk, total - s)) for s in starts]
    return [lambda: lax.fori_loop(0, total, lambda r, carry: (step(r, 1), carry)[1], 0)]


def in_turn(first, second):
    for mine, other in itertools.zip_longest(first, second):
        for thunk in (mine, other):
            if thunk is not None:
                thunk()


def window_tiles(row, flipped, sizes):
    n_row, n_col, tile_rows, tile_cols = sizes
    if not flipped:
        return [row - 1, row, row + 1]
    first = (row * tile_rows - LAYERS + tile_cols) // tile_cols - 1
    starts = [r * tile_rows - LAYERS for r in range(n_row)]
    reach = tile_rows + 2 * LAYERS - 1
    count = max((f + reach) // tile_cols - f // tile_cols + 1 for f in starts)
    return [first + t for t in range(count)]


def selection(row, flipped, start, rows, sizes):
    n_row, n_col, tile_rows, tile_cols = sizes
    inner, outer, limit = (tile_rows, tile_cols, n_col) if flipped else (tile_cols, tile_rows, n_row)
    cells = tile_rows * tile_cols
    shape = (rows, inner, cells)
    major = lax.broadcasted_iota(jnp.int32, shape, 0) + (start + row * tile_rows - LAYERS)
    minor = lax.broadcasted_iota(jnp.int32, shape, 1)
    lane = lax.broadcasted_iota(jnp.int32, shape, 2)
    blocks = []
    for tile in window_tiles(row, flipped, sizes):
        offset = major - tile * outer
        goal = minor * tile_cols + offset if flipped else offset * tile_cols + minor
        ok = (offset >= 0) & (offset < outer) & (major >= 0) & (major < limit * outer)
        block = jnp.where(ok & (lane == goal), 1.0, 0.0)
        blocks.append(block.reshape(rows * inner, cells).astype(jnp.bfloat16))
    return jnp.concatenate(blocks, axis=1)


def split(value, count):
    parts = []
    for _ in range(count):
        part = value.astype(jnp.bfloat16).astype(jnp.float32)
        parts.append(part)
        value = value - part
    return parts


def patch_kernel(tile, sent, *, tile_rows, tile_cols):
    height, span = tile.shape
    cells = tile_rows * tile_cols
    shape = (span, PATCH * cells)
    pixel = lax.broadcasted_iota(jnp.int32, shape, 0)
    lane = lax.broadcasted_iota(jnp.int32, shape, 1)
    goal = (lane % tile_cols) * PATCH + lane // cells
    spread = jnp.where(pixel == goal, 1.0, 0.0).astype(jnp.bfloat16)
    wide = jnp.dot(tile[...].astype(jnp.bfloat16), spread, preferred_element_type=jnp.float32)
    line = lax.broadcasted_iota(jnp.int32, wide.shape, 0) // PATCH
    lane = lax.broadcasted_iota(jnp.int32, wide.shape, 1)
    wide = jnp.where(line == (lane % cells) // tile_cols, wide, 0.0)
    blocks = [wide[:, b * cells : (b + 1) * cells] for b in range(PATCH)]
    stacked = jnp.concatenate(blocks, axis=0).astype(jnp.bfloat16)
    shape = (PATCH * PATCH, PATCH * height)
    pixel = lax.broadcasted_iota(jnp.int32, shape, 0)
    lane = lax.broadcasted_iota(jnp.int32, shape, 1)
    mine = (lane % PATCH == pixel // PATCH) & (lane // height == pixel % PATCH)
    mine = jnp.where(mine, 1.0, 0.0).astype(jnp.bfloat16)
    result = jnp.dot(mine, stacked, preferred_element_type=jnp.float32).astype(jnp.bfloat16)
    sent[...] = jnp.broadcast_to(result[None], sent.shape)


def prepare_kernel(*refs, sizes, count, matrices):
    embed_w, embed_b, conv_w, *others = refs[:count]
    outs = refs[count : count + 2 + matrices]
    kept = refs[count + 2 + matrices : -6]
    conv_w_kept, conv_b, mix_w, mix_b, proj_w, proj_b, up_w, up_b, _, _ = kept
    embed_buf, bias_buf, conv_buf, mix_buf, up_buf, arrived = refs[-6:]
    sources = [embed_w, embed_b, conv_w.at[0], conv_w.at[pl.ds(1, LAYERS - 1)], *others]
    targets = [embed_buf, bias_buf, conv_buf, *kept]
    targets[5], targets[9] = mix_buf, up_buf
    loads = [
        pltpu.make_async_copy(source, target, arrived.at[at])
        for at, (source, target) in enumerate(zip(sources, targets))
    ]
    for load in loads:
        load.start()
    if matrices:
        row = lax.axis_index("row")
        for flipped, target in ((False, outs[2]), (True, outs[3])):
            target[...] = selection(row, flipped, 0, sizes[2] + 2 * LAYERS, sizes)
    for load in loads[:3] + loads[4:5]:
        load.wait()
    embed_w, embed_b = embed_buf, bias_buf
    first_bias = conv_b[0:1, :]
    pixels, width = embed_w.shape
    bias = jnp.concatenate(split(embed_b[...].reshape(1, width), 3), axis=0)
    rest = jnp.zeros((PIECE - pixels - 3, width), jnp.float32)
    left = jnp.concatenate([embed_w[...].astype(jnp.float32), bias, rest], axis=0)
    left = (0.5 * left).astype(jnp.bfloat16)
    products = {}
    for a, b in itertools.product(range(3), range(3)):
        products[a, b] = jnp.dot(left, conv_buf[a, b], preferred_element_type=jnp.float32)
    for flipped, target in ((False, outs[0]), (True, outs[1])):
        for down in range(3):
            pieces, offsets = [], []
            for along in range(3):
                product = products[(along, down) if flipped else (down, along)]
                pieces += split(product[:pixels], 2)
                offset = jnp.sum(product[pixels : pixels + 3], axis=0, keepdims=True)
                if (down, along) == (1, 1):
                    offset = offset + 0.5 * first_bias
                offsets.append(jnp.concatenate(split(offset, 3), axis=0))
                offsets.append(jnp.zeros((SLOT - 3, width), jnp.float32))
            used = 3 * (2 * pixels + SLOT)
            offsets.append(jnp.zeros((width - used, width), jnp.float32))
            value = jnp.concatenate(pieces + offsets, axis=0)
            target[down * width : (down + 1) * width, :] = value.astype(jnp.bfloat16)
    for load in loads[3:4] + loads[5:]:
        load.wait()
    for ref in (conv_w_kept, conv_b, mix_b):
        ref[...] = (0.5 * ref[...].astype(jnp.float32)).astype(ref.dtype)
    quarter = (0.25 * mix_buf[...].astype(jnp.float32)).astype(jnp.bfloat16)
    mix_w[...] = jnp.concatenate([quarter, quarter], axis=0)
    half = (0.5 * up_buf[...].astype(jnp.float32)).astype(jnp.bfloat16)
    joint = jnp.dot(proj_w[...], half, preferred_element_type=jnp.float32)
    up_w[...] = jnp.concatenate(split(joint, 2), axis=0).astype(jnp.bfloat16)
    pieces = jnp.concatenate(split(proj_b[...].reshape(1, -1), 3), axis=0).astype(jnp.bfloat16)
    shift = jnp.dot(pieces, half, preferred_element_type=jnp.float32)
    up_b[...] = 0.5 * up_b[...] + jnp.sum(shift, axis=0)


def encoder_kernel(
    gathered, first_plain, first_turned, *refs, sizes, shared,
):
    n_row, n_col, tile_rows, tile_cols = sizes
    if shared:
        selects = (None, None)
    else:
        selects, refs = refs[:2], refs[2:]
    conv_w, conv_b, mix_w, mix_b, proj_w, proj_b, up_w, up_b, down_w, down_b = refs[:10]
    latents, sym_out, *buffers = refs[10:]
    _, pixels, cells = gathered.shape
    width = mix_w.shape[1]
    span = n_row * tile_rows
    own_rows = latents.shape[0]
    row = lax.axis_index("row")
    col = lax.axis_index("col")

    def keep_inside(value, start, margin):
        rows = value.shape[0]
        if isinstance(start, int):
            edges = [max(0, min(rows, edge - start)) for edge in (margin, margin + tile_rows)]
        else:
            edges = [rows, rows]
        pieces = []
        for low, high in ((0, edges[0]), (edges[1], rows)):
            first = row * tile_rows - margin + start + low
            lines = [
                jnp.where((first + r >= 0) & (first + r < span), value[low + r], 0.0)[None]
                for r in range(high - low)
            ]
            pieces.append(lines)
        inner = [value[edges[0] : edges[1]]] if edges[1] > edges[0] else []
        return jnp.concatenate(pieces[0] + inner + pieces[1], axis=0)

    def shifted(stage, start, value):
        count = value.shape[0]
        base = 0 if shared else start
        stage[pl.ds(base, count), PAD : PAD + span, :] = value
        return [
            stage[pl.ds(base, count), PAD - 1 + at : PAD - 1 + at + span, :] for at in range(3)
        ]

    def emit(pair, start, value):
        target, stage = pair
        for at, part in enumerate(shifted(stage, start, value)):
            lanes = slice(at * width, (at + 1) * width)
            target[pl.ds(start, value.shape[0]), :, lanes] = part.astype(jnp.bfloat16)

    def patches(pair, flipped):
        target, stage = pair
        group, inner = (n_row, tile_rows) if flipped else (n_col, tile_cols)
        limit = (n_col if flipped else n_row) - 1
        ones = jnp.ones((width - 6 * pixels, cells), jnp.bfloat16)
        columns = []
        for tile in window_tiles(row, flipped, sizes):
            at = jnp.clip(tile, 0, limit)
            stacked = []
            for g in range(group):
                source = gathered[at * n_row + g] if flipped else gathered[g * n_row + at]
                stacked += [source] * 6 + [ones]
            columns.append(jnp.concatenate(stacked, axis=0))
        source = jnp.concatenate(columns, axis=1)

        def step(start, rows):
            if shared:
                select = selection(row, flipped, start, rows, sizes)
            else:
                select = selects[flipped][start * inner : (start + rows) * inner, :]
            value = lax.dot_general(
                select, source, (((1,), (1,)), ((), ())), preferred_element_type=jnp.float32
            )
            value = jnp.concatenate(
                [
                    value[:, g * width : (g + 1) * width].reshape(rows, inner, width)
                    for g in range(group)
                ],
                axis=1,
            )
            before, same, after = shifted(stage, start, value)
            lane = lax.broadcasted_iota(jnp.int32, same.shape, 2)
            which = jnp.where(lane < 6 * pixels, lane // (2 * pixels), (lane - 6 * pixels) // SLOT)
            value = jnp.where(which == 0, before, jnp.where(which == 1, same, after))
            target[pl.ds(start, rows), :, :] = value.astype(jnp.bfloat16)

        return row_steps(tile_rows + 2 * LAYERS, span, step)

    def taps(layer, flipped):
        if layer == 0:
            return (first_turned if flipped else first_plain)[...]
        if flipped:
            blocks = [conv_w[layer - 1, :, a].reshape(3 * width, width) for a in range(3)]
            return jnp.concatenate(blocks, axis=0)
        return conv_w[layer - 1].reshape(9 * width, width)

    def convolve(source, layer, flipped, start, rows, place, extent):
        windows = [
            source[pl.ds(start + a, rows), pl.ds(place, extent), :].reshape(rows * extent, -1)
            for a in range(3)
        ]
        total = jnp.dot(
            jnp.concatenate(windows, axis=1),
            taps(layer, flipped),
            preferred_element_type=jnp.float32,
        )
        if layer > 0:
            total = total + conv_b[layer : layer + 1, :]
        return gelu_of_twice(total).reshape(rows, extent, width)

    def layer_steps(layer, flipped, source, target):
        def step(start, rows):
            value = convolve(source[0], layer, flipped, start, rows, 0, span)
            emit(target, start, keep_inside(value, start, LAYERS - layer - 1))

        return row_steps(tile_rows + 2 * (LAYERS - layer - 1), span, step)

    def last_layer(flipped, source):
        place = pl.multiple_of(col * tile_cols, tile_cols)
        windows = [
            jnp.concatenate(
                [
                    source[0][pl.ds(col * own_rows + a, own_rows), :, :].reshape(own_rows * span, -1),
                    source[0][a : a + tile_rows, pl.ds(place, tile_cols), :].reshape(cells, -1),
                ],
                axis=0,
            )
            for a in range(3)
        ]
        total = jnp.dot(
            jnp.concatenate(windows, axis=1),
            taps(LAYERS - 1, flipped),
            preferred_element_type=jnp.float32,
        )
        total = gelu_of_twice(total + conv_b[LAYERS - 1 :, :]).astype(jnp.bfloat16)
        strip = total[: own_rows * span].reshape(own_rows, span, width)
        return strip, total[own_rows * span :].reshape(tile_rows, tile_cols, width)

    def average(first, second):
        total = first.astype(jnp.float32) + second.astype(jnp.float32)
        return (total * 0.5).astype(jnp.bfloat16)

    half = len(buffers) // 2
    pairs = list(zip(buffers[:half], buffers[half:]))
    for _, stage in pairs:
        stage[:, :PAD, :] = jnp.zeros((stage.shape[0], PAD, width), jnp.float32)
        stage[:, PAD + span :, :] = jnp.zeros((stage.shape[0], PAD, width), jnp.float32)
    plain, turned = pairs[:LAYERS], pairs[-LAYERS:]
    if shared:
        strips, tiles = [], []
        for flipped, chain in ((False, plain), (True, turned)):
            steps = patches(chain[0], flipped)
            for layer in range(LAYERS - 1):
                steps += layer_steps(layer, flipped, chain[layer], chain[layer + 1])
            for thunk in steps:
                thunk()
            strip, tile = last_layer(flipped, chain[-1])
            strips.append(strip)
            tiles.append(tile)
    else:
        in_turn(patches(plain[0], False), patches(turned[0], True))
        in_turn(
            layer_steps(0, False, plain[0], plain[1]), layer_steps(0, True, turned[0], turned[1])
        )
        for layer in range(1, LAYERS - 1):
            in_turn(
                layer_steps(layer, False, plain[layer], plain[layer + 1]),
                layer_steps(layer, True, turned[layer], turned[layer + 1]),
            )
        strips, tiles = zip(last_layer(False, plain[-1]), last_layer(True, turned[-1]))
    sym_out[...] = average(*tiles)
    both = jnp.concatenate([s.reshape(own_rows * span, width) for s in strips], axis=1)
    mixed = jnp.dot(both, mix_w[...], preferred_element_type=jnp.float32) + mix_b[...].reshape(1, width)
    summed = jnp.sum(gelu_of_twice(mixed).reshape(own_rows, span, width), axis=1)
    pooled = (summed / span).astype(jnp.bfloat16)
    latent = jnp.dot(pooled, proj_w[...], preferred_element_type=jnp.float32)
    latent = latent + proj_b[...].reshape(1, -1)
    twice = jnp.concatenate([pooled, pooled], axis=1)
    hidden = jnp.dot(twice, up_w[...], preferred_element_type=jnp.float32)
    hidden = gelu_of_twice(hidden + up_b[...].reshape(1, -1)).astype(jnp.bfloat16)
    result = jnp.dot(hidden, down_w[...], preferred_element_type=jnp.float32)
    latents[...] = (latent + result + down_b[...].reshape(1, -1)).astype(jnp.bfloat16)


def body(contact_map, embed_weight, embed_bias, conv_weight, *rest):
    n_row, n_col = lax.axis_size("row"), lax.axis_size("col")
    tile_rows = contact_map.shape[0] // PATCH
    tile_cols = contact_map.shape[1] // PATCH
    sizes = (n_row, n_col, tile_rows, tile_cols)
    pixels, width = embed_weight.shape
    cells = tile_rows * tile_cols
    span = n_row * tile_rows
    own_rows = tile_rows // n_col
    out_width = rest[-1].shape[0]
    heights = [tile_rows + 2 * (LAYERS - layer) for layer in range(LAYERS)]
    shared = sum(heights) * span > UNROLL_CELLS * 2
    whole = pl.BlockSpec(memory_space=pltpu.VMEM)

    def near(value):
        return pltpu.with_memory_space_constraint(value, pltpu.VMEM)

    shape = (n_row * n_col, pixels, cells)
    sent = pl.pallas_call(
        functools.partial(patch_kernel, tile_rows=tile_rows, tile_cols=tile_cols),
        out_shape=(jax.ShapeDtypeStruct if shared else pltpu.VMEM)(shape, jnp.bfloat16),
        in_specs=[whole],
        out_specs=whole,
        name="patches",
    )(contact_map)
    gathered = lax.all_to_all(sent, ("col", "row"), 0, 0, tiled=True)
    shapes = [(3 * width, width)] * 2
    if not shared:
        turned_tiles = len(window_tiles(0, True, sizes))
        shapes.append((heights[0] * tile_cols, 3 * cells))
        shapes.append((heights[0] * tile_rows, turned_tiles * cells))
    shapes = [pltpu.VMEM(shape, jnp.bfloat16) for shape in shapes]
    matrices = len(shapes) - 2
    later = (LAYERS - 1,) + conv_weight.shape[1:]
    shapes.append(pltpu.VMEM(later, conv_weight.dtype))
    shapes += [pltpu.VMEM(value.shape, value.dtype) for value in rest]
    mix_weight, up_weight = rest[1], rest[5]
    shapes[matrices + 4] = pltpu.VMEM((2 * width, width), jnp.bfloat16)
    shapes[matrices + 8] = pltpu.VMEM((2 * width, up_weight.shape[1]), jnp.bfloat16)
    inputs = (embed_weight, embed_bias, conv_weight, *rest)
    prepared = pl.pallas_call(
        functools.partial(prepare_kernel, sizes=sizes, count=len(inputs), matrices=matrices),
        out_shape=shapes,
        in_specs=[pl.BlockSpec(memory_space=pl.ANY)] * len(inputs),
        out_specs=[whole] * len(shapes),
        scratch_shapes=[
            pltpu.VMEM(embed_weight.shape, embed_weight.dtype),
            pltpu.VMEM(embed_bias.shape, embed_bias.dtype),
            pltpu.VMEM(conv_weight.shape[1:], conv_weight.dtype),
            pltpu.VMEM(mix_weight.shape, mix_weight.dtype),
            pltpu.VMEM(up_weight.shape, up_weight.dtype),
            pltpu.SemaphoreType.DMA((len(inputs) + 1,)),
        ],
        name="prepare",
    )(*inputs)
    prepared = [near(value) for value in prepared]
    operands = [gathered if shared else near(gathered), *prepared]
    in_specs = [whole] * len(operands)
    buffers = [
        pltpu.VMEM((h, span, width * (3 if at else 1)), jnp.bfloat16) for at, h in enumerate(heights)
    ]
    stages = [
        pltpu.VMEM((1 if shared else h, span + 2 * PAD, width), jnp.float32) for h in heights
    ]
    if not shared:
        buffers, stages = buffers * 2, stages * 2
    return pl.pallas_call(
        functools.partial(encoder_kernel, sizes=sizes, shared=shared),
        out_shape=(
            jax.ShapeDtypeStruct((own_rows, out_width), jnp.bfloat16),
            jax.ShapeDtypeStruct((tile_rows, tile_cols, width), jnp.bfloat16),
        ),
        in_specs=in_specs,
        out_specs=(whole, whole),
        scratch_shapes=buffers + stages,
        name="encoder",
    )(*operands)


def solution(mesh):
    return jax.shard_map(
        body,
        mesh=mesh,
        in_specs=(P("row", "col"), P(), P(), P(), P(), P(), P(), P(), P(), P(), P(), P(), P()),
        out_specs=(P(("row", "col"), None), P("row", "col", None)),
        check_vma=False,
    )
```

```python
import functools
import itertools

import jax
import jax.numpy as jnp
from jax import lax
from jax.experimental import pallas as pl
from jax.experimental.pallas import tpu as pltpu
from jax.sharding import PartitionSpec as P

PATCH = 4
LAYERS = 3
UNROLL_CELLS = 2048
CHUNK_CELLS = 1024
PAD = 8
PIECE = 32
SLOT = 8


def gelu_of_twice(half):
    scale = 2 * 0.7978845608028654
    return half + half * jnp.tanh(half * (scale + (4 * scale * 0.044715) * (half * half)))


def row_steps(total, span, step):
    if total * span <= UNROLL_CELLS:
        chunk = max(1, CHUNK_CELLS // span)
        starts = range(0, total, chunk)
        return [functools.partial(step, s, min(chunk, total - s)) for s in starts]
    return [lambda: lax.fori_loop(0, total, lambda r, carry: (step(r, 1), carry)[1], 0)]


def in_turn(first, second):
    for mine, other in itertools.zip_longest(first, second):
        for thunk in (mine, other):
            if thunk is not None:
                thunk()


def window_tiles(row, flipped, sizes):
    n_row, n_col, tile_rows, tile_cols = sizes
    if not flipped:
        return [row - 1, row, row + 1]
    first = (row * tile_rows - LAYERS + tile_cols) // tile_cols - 1
    starts = [r * tile_rows - LAYERS for r in range(n_row)]
    reach = tile_rows + 2 * LAYERS - 1
    count = max((f + reach) // tile_cols - f // tile_cols + 1 for f in starts)
    return [first + t for t in range(count)]


def selection(row, flipped, start, rows, sizes):
    n_row, n_col, tile_rows, tile_cols = sizes
    inner, outer, limit = (tile_rows, tile_cols, n_col) if flipped else (tile_cols, tile_rows, n_row)
    cells = tile_rows * tile_cols
    shape = (rows, inner, cells)
    major = lax.broadcasted_iota(jnp.int32, shape, 0) + (start + row * tile_rows - LAYERS)
    minor = lax.broadcasted_iota(jnp.int32, shape, 1)
    lane = lax.broadcasted_iota(jnp.int32, shape, 2)
    blocks = []
    for tile in window_tiles(row, flipped, sizes):
        offset = major - tile * outer
        goal = minor * tile_cols + offset if flipped else offset * tile_cols + minor
        ok = (offset >= 0) & (offset < outer) & (major >= 0) & (major < limit * outer)
        block = jnp.where(ok & (lane == goal), 1.0, 0.0)
        blocks.append(block.reshape(rows * inner, cells))
    if not flipped:
        blocks = [blocks[1], blocks[0] + blocks[2]]
    return jnp.concatenate([block.astype(jnp.bfloat16) for block in blocks], axis=1)


def split(value, count):
    parts = []
    for _ in range(count):
        part = value.astype(jnp.bfloat16).astype(jnp.float32)
        parts.append(part)
        value = value - part
    return parts


def patch_kernel(tile, sent, *, tile_rows, tile_cols):
    height, span = tile.shape
    cells = tile_rows * tile_cols
    shape = (span, PATCH * cells)
    pixel = lax.broadcasted_iota(jnp.int32, shape, 0)
    lane = lax.broadcasted_iota(jnp.int32, shape, 1)
    goal = (lane % tile_cols) * PATCH + lane // cells
    spread = jnp.where(pixel == goal, 1.0, 0.0).astype(jnp.bfloat16)
    wide = jnp.dot(tile[...].astype(jnp.bfloat16), spread, preferred_element_type=jnp.float32)
    line = lax.broadcasted_iota(jnp.int32, wide.shape, 0) // PATCH
    lane = lax.broadcasted_iota(jnp.int32, wide.shape, 1)
    wide = jnp.where(line == (lane % cells) // tile_cols, wide, 0.0)
    blocks = [wide[:, b * cells : (b + 1) * cells] for b in range(PATCH)]
    stacked = jnp.concatenate(blocks, axis=0).astype(jnp.bfloat16)
    shape = (PATCH * PATCH, PATCH * height)
    pixel = lax.broadcasted_iota(jnp.int32, shape, 0)
    lane = lax.broadcasted_iota(jnp.int32, shape, 1)
    mine = (lane % PATCH == pixel // PATCH) & (lane // height == pixel % PATCH)
    mine = jnp.where(mine, 1.0, 0.0).astype(jnp.bfloat16)
    result = jnp.dot(mine, stacked, preferred_element_type=jnp.float32).astype(jnp.bfloat16)
    sent[...] = jnp.broadcast_to(result[None], sent.shape)


def prepare_kernel(*refs, sizes, count, matrices):
    embed_w, embed_b, conv_w, *others = refs[:count]
    outs = refs[count : count + 2 + matrices]
    kept = refs[count + 2 + matrices : -6]
    conv_w_kept, conv_b, mix_w, mix_b, proj_w, proj_b, up_w, up_b, _, _ = kept
    embed_buf, bias_buf, conv_buf, mix_buf, up_buf, arrived = refs[-6:]
    sources = [embed_w, embed_b, conv_w.at[0], conv_w.at[pl.ds(1, LAYERS - 1)], *others]
    targets = [embed_buf, bias_buf, conv_buf, *kept]
    targets[5], targets[9] = mix_buf, up_buf
    loads = [
        pltpu.make_async_copy(source, target, arrived.at[at])
        for at, (source, target) in enumerate(zip(sources, targets))
    ]
    for load in loads:
        load.start()
    if matrices:
        row = lax.axis_index("row")
        for flipped, target in ((False, outs[2]), (True, outs[3])):
            target[...] = selection(row, flipped, 0, sizes[2] + 2 * LAYERS, sizes)
    for load in loads[:3] + loads[4:5]:
        load.wait()
    embed_w, embed_b = embed_buf, bias_buf
    first_bias = conv_b[0:1, :]
    pixels, width = embed_w.shape
    bias = jnp.concatenate(split(embed_b[...].reshape(1, width), 3), axis=0)
    rest = jnp.zeros((PIECE - pixels - 3, width), jnp.float32)
    left = jnp.concatenate([embed_w[...].astype(jnp.float32), bias, rest], axis=0)
    left = (0.5 * left).astype(jnp.bfloat16)
    products = {}
    for a, b in itertools.product(range(3), range(3)):
        products[a, b] = jnp.dot(left, conv_buf[a, b], preferred_element_type=jnp.float32)
    for flipped, target in ((False, outs[0]), (True, outs[1])):
        for down in range(3):
            pieces, offsets = [], []
            for along in range(3):
                product = products[(along, down) if flipped else (down, along)]
                pieces += split(product[:pixels], 2)
                offset = jnp.sum(product[pixels : pixels + 3], axis=0, keepdims=True)
                if (down, along) == (1, 1):
                    offset = offset + 0.5 * first_bias
                offsets.append(jnp.concatenate(split(offset, 3), axis=0))
                offsets.append(jnp.zeros((SLOT - 3, width), jnp.float32))
            used = 3 * (2 * pixels + SLOT)
            offsets.append(jnp.zeros((width - used, width), jnp.float32))
            value = jnp.concatenate(pieces + offsets, axis=0)
            target[down * width : (down + 1) * width, :] = value.astype(jnp.bfloat16)
    for load in loads[3:4] + loads[5:]:
        load.wait()
    for ref in (conv_w_kept, conv_b, mix_b):
        ref[...] = (0.5 * ref[...].astype(jnp.float32)).astype(ref.dtype)
    quarter = (0.25 * mix_buf[...].astype(jnp.float32)).astype(jnp.bfloat16)
    mix_w[...] = jnp.concatenate([quarter, quarter], axis=0)
    half = (0.5 * up_buf[...].astype(jnp.float32)).astype(jnp.bfloat16)
    joint = jnp.dot(proj_w[...], half, preferred_element_type=jnp.float32)
    up_w[...] = jnp.concatenate(split(joint, 2), axis=0).astype(jnp.bfloat16)
    pieces = jnp.concatenate(split(proj_b[...].reshape(1, -1), 3), axis=0).astype(jnp.bfloat16)
    shift = jnp.dot(pieces, half, preferred_element_type=jnp.float32)
    up_b[...] = 0.5 * up_b[...] + jnp.sum(shift, axis=0)


def encoder_kernel(
    gathered, first_plain, first_turned, *refs, sizes, shared,
):
    n_row, n_col, tile_rows, tile_cols = sizes
    if shared:
        selects = (None, None)
    else:
        selects, refs = refs[:2], refs[2:]
    conv_w, conv_b, mix_w, mix_b, proj_w, proj_b, up_w, up_b, down_w, down_b = refs[:10]
    latents, sym_out, *buffers = refs[10:]
    _, pixels, cells = gathered.shape
    width = mix_w.shape[1]
    span = n_row * tile_rows
    own_rows = latents.shape[0]
    row = lax.axis_index("row")
    col = lax.axis_index("col")

    def keep_inside(value, start, margin):
        rows = value.shape[0]
        if isinstance(start, int):
            edges = [max(0, min(rows, edge - start)) for edge in (margin, margin + tile_rows)]
        else:
            edges = [rows, rows]
        pieces = []
        for low, high in ((0, edges[0]), (edges[1], rows)):
            first = row * tile_rows - margin + start + low
            lines = [
                jnp.where((first + r >= 0) & (first + r < span), value[low + r], 0.0)[None]
                for r in range(high - low)
            ]
            pieces.append(lines)
        inner = [value[edges[0] : edges[1]]] if edges[1] > edges[0] else []
        return jnp.concatenate(pieces[0] + inner + pieces[1], axis=0)

    def shifted(stage, start, value):
        count = value.shape[0]
        base = 0 if shared else start
        stage[pl.ds(base, count), PAD : PAD + span, :] = value
        return [
            stage[pl.ds(base, count), PAD - 1 + at : PAD - 1 + at + span, :] for at in range(3)
        ]

    def emit(pair, start, value):
        target, stage = pair
        for at, part in enumerate(shifted(stage, start, value)):
            lanes = slice(at * width, (at + 1) * width)
            target[pl.ds(start, value.shape[0]), :, lanes] = part.astype(jnp.bfloat16)

    def patches(pair, flipped):
        target, stage = pair
        group, inner = (n_row, tile_rows) if flipped else (n_col, tile_cols)
        limit = (n_col if flipped else n_row) - 1
        ones = jnp.ones((width - 6 * pixels, cells), jnp.bfloat16)
        columns = [[] for _ in window_tiles(row, flipped, sizes)]
        for column, tile in zip(columns, window_tiles(row, flipped, sizes)):
            at = jnp.clip(tile, 0, limit)
            for g in range(group):
                column.append(gathered[at * n_row + g] if flipped else gathered[g * n_row + at])
        if not flipped:
            lane = lax.broadcasted_iota(jnp.int32, (pixels, cells), 1)
            late = lane >= (tile_rows - LAYERS) * tile_cols
            rims = [
                jnp.where(late, up.astype(jnp.float32), down.astype(jnp.float32))
                for up, down in zip(columns[0], columns[2])
            ]
            columns = [columns[1], [rim.astype(jnp.bfloat16) for rim in rims]]
        columns = [
            jnp.concatenate([part for tile in column for part in [tile] * 6 + [ones]], axis=0)
            for column in columns
        ]
        source = jnp.concatenate(columns, axis=1)

        def step(start, rows):
            if shared:
                select = selection(row, flipped, start, rows, sizes)
            else:
                select = selects[flipped][start * inner : (start + rows) * inner, :]
            value = lax.dot_general(
                select, source, (((1,), (1,)), ((), ())), preferred_element_type=jnp.float32
            )
            value = jnp.concatenate(
                [
                    value[:, g * width : (g + 1) * width].reshape(rows, inner, width)
                    for g in range(group)
                ],
                axis=1,
            )
            before, same, after = shifted(stage, start, value)
            lane = lax.broadcasted_iota(jnp.int32, same.shape, 2)
            which = jnp.where(lane < 6 * pixels, lane // (2 * pixels), (lane - 6 * pixels) // SLOT)
            value = jnp.where(which == 0, before, jnp.where(which == 1, same, after))
            target[pl.ds(start, rows), :, :] = value.astype(jnp.bfloat16)

        return row_steps(tile_rows + 2 * LAYERS, span, step)

    def taps(layer, flipped):
        if layer == 0:
            return (first_turned if flipped else first_plain)[...]
        if flipped:
            blocks = [conv_w[layer - 1, :, a].reshape(3 * width, width) for a in range(3)]
            return jnp.concatenate(blocks, axis=0)
        return conv_w[layer - 1].reshape(9 * width, width)

    def convolve(source, layer, flipped, start, rows, place, extent):
        windows = [
            source[pl.ds(start + a, rows), pl.ds(place, extent), :].reshape(rows * extent, -1)
            for a in range(3)
        ]
        total = jnp.dot(
            jnp.concatenate(windows, axis=1),
            taps(layer, flipped),
            preferred_element_type=jnp.float32,
        )
        if layer > 0:
            total = total + conv_b[layer : layer + 1, :]
        return gelu_of_twice(total).reshape(rows, extent, width)

    def layer_steps(layer, flipped, source, target):
        def step(start, rows):
            value = convolve(source[0], layer, flipped, start, rows, 0, span)
            emit(target, start, keep_inside(value, start, LAYERS - layer - 1))

        return row_steps(tile_rows + 2 * (LAYERS - layer - 1), span, step)

    def last_strip(flipped, source):
        strip = convolve(source[0], LAYERS - 1, flipped, col * own_rows, own_rows, 0, span)
        return strip.astype(jnp.bfloat16)

    def last_tile(flipped, source):
        place = pl.multiple_of(col * tile_cols, tile_cols)
        tile = convolve(source[0], LAYERS - 1, flipped, 0, tile_rows, place, tile_cols)
        return tile.astype(jnp.bfloat16)

    def average(first, second):
        total = first.astype(jnp.float32) + second.astype(jnp.float32)
        return (total * 0.5).astype(jnp.bfloat16)

    half = len(buffers) // 2
    pairs = list(zip(buffers[:half], buffers[half:]))
    for _, stage in pairs:
        stage[:, :PAD, :] = jnp.zeros((stage.shape[0], PAD, width), jnp.float32)
        stage[:, PAD + span :, :] = jnp.zeros((stage.shape[0], PAD, width), jnp.float32)
    plain, turned = pairs[:LAYERS], pairs[-LAYERS:]
    if shared:
        strips, tiles = [], []
        for flipped, chain in ((False, plain), (True, turned)):
            steps = patches(chain[0], flipped)
            for layer in range(LAYERS - 1):
                steps += layer_steps(layer, flipped, chain[layer], chain[layer + 1])
            for thunk in steps:
                thunk()
            strips.append(last_strip(flipped, chain[-1]))
            tiles.append(last_tile(flipped, chain[-1]))
    else:
        in_turn(patches(plain[0], False), patches(turned[0], True))
        in_turn(layer_steps(0, False, plain[0], plain[1]), [])
        in_turn(layer_steps(0, True, turned[0], turned[1]), [])
        in_turn(layer_steps(1, False, plain[1], plain[2]), [])
        in_turn(layer_steps(1, True, turned[1], turned[2]), [])
        strip_m = last_strip(False, plain[-1])
        tile_m = last_tile(False, plain[-1])
        strip_t = last_strip(True, turned[-1])
        tile_t = last_tile(True, turned[-1])
        strips, tiles = [strip_m, strip_t], [tile_m, tile_t]
    sym_out[...] = average(*tiles)
    both = jnp.concatenate([s.reshape(own_rows * span, width) for s in strips], axis=1)
    mixed = jnp.dot(both, mix_w[...], preferred_element_type=jnp.float32) + mix_b[...].reshape(1, width)
    summed = jnp.sum(gelu_of_twice(mixed).reshape(own_rows, span, width), axis=1)
    pooled = (summed / span).astype(jnp.bfloat16)
    latent = jnp.dot(pooled, proj_w[...], preferred_element_type=jnp.float32)
    latent = latent + proj_b[...].reshape(1, -1)
    twice = jnp.concatenate([pooled, pooled], axis=1)
    hidden = jnp.dot(twice, up_w[...], preferred_element_type=jnp.float32)
    hidden = gelu_of_twice(hidden + up_b[...].reshape(1, -1)).astype(jnp.bfloat16)
    result = jnp.dot(hidden, down_w[...], preferred_element_type=jnp.float32)
    latents[...] = (latent + result + down_b[...].reshape(1, -1)).astype(jnp.bfloat16)


def body(contact_map, embed_weight, embed_bias, conv_weight, *rest):
    n_row, n_col = lax.axis_size("row"), lax.axis_size("col")
    tile_rows = contact_map.shape[0] // PATCH
    tile_cols = contact_map.shape[1] // PATCH
    sizes = (n_row, n_col, tile_rows, tile_cols)
    pixels, width = embed_weight.shape
    cells = tile_rows * tile_cols
    span = n_row * tile_rows
    own_rows = tile_rows // n_col
    out_width = rest[-1].shape[0]
    heights = [tile_rows + 2 * (LAYERS - layer) for layer in range(LAYERS)]
    shared = sum(heights) * span > UNROLL_CELLS * 2
    whole = pl.BlockSpec(memory_space=pltpu.VMEM)

    def near(value):
        return pltpu.with_memory_space_constraint(value, pltpu.VMEM)

    shape = (n_row * n_col, pixels, cells)
    sent = pl.pallas_call(
        functools.partial(patch_kernel, tile_rows=tile_rows, tile_cols=tile_cols),
        out_shape=(jax.ShapeDtypeStruct if shared else pltpu.VMEM)(shape, jnp.bfloat16),
        in_specs=[whole],
        out_specs=whole,
        name="patches",
    )(contact_map)
    gathered = lax.all_to_all(sent, ("col", "row"), 0, 0, tiled=True)
    shapes = [(3 * width, width)] * 2
    if not shared:
        turned_tiles = len(window_tiles(0, True, sizes))
        shapes.append((heights[0] * tile_cols, 2 * cells))
        shapes.append((heights[0] * tile_rows, turned_tiles * cells))
    shapes = [pltpu.VMEM(shape, jnp.bfloat16) for shape in shapes]
    matrices = len(shapes) - 2
    later = (LAYERS - 1,) + conv_weight.shape[1:]
    shapes.append(pltpu.VMEM(later, conv_weight.dtype))
    shapes += [pltpu.VMEM(value.shape, value.dtype) for value in rest]
    mix_weight, up_weight = rest[1], rest[5]
    shapes[matrices + 4] = pltpu.VMEM((2 * width, width), jnp.bfloat16)
    shapes[matrices + 8] = pltpu.VMEM((2 * width, up_weight.shape[1]), jnp.bfloat16)
    inputs = (embed_weight, embed_bias, conv_weight, *rest)
    prepared = pl.pallas_call(
        functools.partial(prepare_kernel, sizes=sizes, count=len(inputs), matrices=matrices),
        out_shape=shapes,
        in_specs=[pl.BlockSpec(memory_space=pl.ANY)] * len(inputs),
        out_specs=[whole] * len(shapes),
        scratch_shapes=[
            pltpu.VMEM(embed_weight.shape, embed_weight.dtype),
            pltpu.VMEM(embed_bias.shape, embed_bias.dtype),
            pltpu.VMEM(conv_weight.shape[1:], conv_weight.dtype),
            pltpu.VMEM(mix_weight.shape, mix_weight.dtype),
            pltpu.VMEM(up_weight.shape, up_weight.dtype),
            pltpu.SemaphoreType.DMA((len(inputs) + 1,)),
        ],
        name="prepare",
    )(*inputs)
    prepared = [near(value) for value in prepared]
    operands = [gathered if shared else near(gathered), *prepared]
    in_specs = [whole] * len(operands)
    buffers = [
        pltpu.VMEM((h, span, width * (3 if at else 1)), jnp.bfloat16) for at, h in enumerate(heights)
    ]
    stages = [
        pltpu.VMEM((1 if shared else h, span + 2 * PAD, width), jnp.float32) for h in heights
    ]
    if not shared:
        buffers, stages = buffers * 2, stages * 2
    return pl.pallas_call(
        functools.partial(encoder_kernel, sizes=sizes, shared=shared),
        out_shape=(
            jax.ShapeDtypeStruct((own_rows, out_width), jnp.bfloat16),
            jax.ShapeDtypeStruct((tile_rows, tile_cols, width), jnp.bfloat16),
        ),
        in_specs=in_specs,
        out_specs=(whole, whole),
        scratch_shapes=buffers + stages,
        name="encoder",
    )(*operands)


def solution(mesh):
    return jax.shard_map(
        body,
        mesh=mesh,
        in_specs=(P("row", "col"), P(), P(), P(), P(), P(), P(), P(), P(), P(), P(), P(), P()),
        out_specs=(P(("row", "col"), None), P("row", "col", None)),
        check_vma=False,
    )
```

```python
import functools
import itertools

import jax
import jax.numpy as jnp
from jax import lax
from jax.experimental import pallas as pl
from jax.experimental.pallas import tpu as pltpu
from jax.sharding import PartitionSpec as P

PATCH = 4
LAYERS = 3
UNROLL_CELLS = 2048
CHUNK_CELLS = 1024
PAD = 8
PIECE = 32
SLOT = 8


def gelu_of_twice(half):
    scale = 2 * 0.7978845608028654
    return half + half * jnp.tanh(half * (scale + (4 * scale * 0.044715) * (half * half)))


def row_steps(total, span, step):
    if total * span <= UNROLL_CELLS:
        chunk = max(1, CHUNK_CELLS // span)
        starts = range(0, total, chunk)
        return [functools.partial(step, s, min(chunk, total - s)) for s in starts]
    return [lambda: lax.fori_loop(0, total, lambda r, carry: (step(r, 1), carry)[1], 0)]


def in_turn(first, second):
    for mine, other in itertools.zip_longest(first, second):
        for thunk in (mine, other):
            if thunk is not None:
                thunk()


def window_tiles(row, flipped, sizes):
    n_row, n_col, tile_rows, tile_cols = sizes
    if not flipped:
        return [row - 1, row, row + 1]
    first = (row * tile_rows - LAYERS + tile_cols) // tile_cols - 1
    starts = [r * tile_rows - LAYERS for r in range(n_row)]
    reach = tile_rows + 2 * LAYERS - 1
    count = max((f + reach) // tile_cols - f // tile_cols + 1 for f in starts)
    return [first + t for t in range(count)]


def selection(row, flipped, start, rows, sizes):
    n_row, n_col, tile_rows, tile_cols = sizes
    inner, outer, limit = (tile_rows, tile_cols, n_col) if flipped else (tile_cols, tile_rows, n_row)
    cells = tile_rows * tile_cols
    shape = (rows, inner, cells)
    major = lax.broadcasted_iota(jnp.int32, shape, 0) + (start + row * tile_rows - LAYERS)
    minor = lax.broadcasted_iota(jnp.int32, shape, 1)
    lane = lax.broadcasted_iota(jnp.int32, shape, 2)
    blocks = []
    for tile in window_tiles(row, flipped, sizes):
        offset = major - tile * outer
        goal = minor * tile_cols + offset if flipped else offset * tile_cols + minor
        ok = (offset >= 0) & (offset < outer) & (major >= 0) & (major < limit * outer)
        block = jnp.where(ok & (lane == goal), 1.0, 0.0)
        blocks.append(block.reshape(rows * inner, cells))
    if not flipped:
        blocks = [blocks[1], blocks[0] + blocks[2]]
    return jnp.concatenate([block.astype(jnp.bfloat16) for block in blocks], axis=1)


def split(value, count):
    parts = []
    for _ in range(count):
        part = value.astype(jnp.bfloat16).astype(jnp.float32)
        parts.append(part)
        value = value - part
    return parts


def patch_kernel(tile, sent, *, tile_rows, tile_cols):
    height, span = tile.shape
    cells = tile_rows * tile_cols
    shape = (span, PATCH * cells)
    pixel = lax.broadcasted_iota(jnp.int32, shape, 0)
    lane = lax.broadcasted_iota(jnp.int32, shape, 1)
    goal = (lane % tile_cols) * PATCH + lane // cells
    spread = jnp.where(pixel == goal, 1.0, 0.0).astype(jnp.bfloat16)
    wide = jnp.dot(tile[...].astype(jnp.bfloat16), spread, preferred_element_type=jnp.float32)
    line = lax.broadcasted_iota(jnp.int32, wide.shape, 0) // PATCH
    lane = lax.broadcasted_iota(jnp.int32, wide.shape, 1)
    wide = jnp.where(line == (lane % cells) // tile_cols, wide, 0.0)
    pair = 2 * PATCH
    summed = sum(wide[at : at + pair] for at in range(pair, height, pair)) + wide[:pair]
    summed = summed[:PATCH] + summed[PATCH:]
    blocks = [summed[:, b * cells : (b + 1) * cells] for b in range(PATCH)]
    result = jnp.concatenate(blocks, axis=0).astype(jnp.bfloat16)
    sent[...] = jnp.broadcast_to(result[None], sent.shape)


def prepare_kernel(*refs, sizes, count, matrices):
    embed_w, embed_b, conv_w, *others = refs[:count]
    outs = refs[count : count + 2 + matrices]
    kept = refs[count + 2 + matrices : -6]
    conv_w_kept, conv_b, mix_w, mix_b, proj_w, proj_b, up_w, up_b, _, _ = kept
    embed_buf, bias_buf, conv_buf, mix_buf, up_buf, arrived = refs[-6:]
    sources = [embed_w, embed_b, conv_w.at[0], conv_w.at[pl.ds(1, LAYERS - 1)], *others]
    targets = [embed_buf, bias_buf, conv_buf, *kept]
    targets[5], targets[9] = mix_buf, up_buf
    loads = [
        pltpu.make_async_copy(source, target, arrived.at[at])
        for at, (source, target) in enumerate(zip(sources, targets))
    ]
    for load in loads:
        load.start()
    if matrices:
        row = lax.axis_index("row")
        for flipped, target in ((False, outs[2]), (True, outs[3])):
            target[...] = selection(row, flipped, 0, sizes[2] + 2 * LAYERS, sizes)
    for load in loads[:3] + loads[4:5]:
        load.wait()
    embed_w, embed_b = embed_buf, bias_buf
    first_bias = conv_b[0:1, :]
    pixels, width = embed_w.shape
    bias = jnp.concatenate(split(embed_b[...].reshape(1, width), 3), axis=0)
    rest = jnp.zeros((PIECE - pixels - 3, width), jnp.float32)
    lines = embed_w[...].astype(jnp.float32)
    order = [PATCH * a + b for b in range(PATCH) for a in range(PATCH)]
    left = jnp.concatenate([lines[p : p + 1] for p in order] + [bias, rest], axis=0)
    left = (0.5 * left).astype(jnp.bfloat16)
    products = {}
    for a, b in itertools.product(range(3), range(3)):
        products[a, b] = jnp.dot(left, conv_buf[a, b], preferred_element_type=jnp.float32)
    for flipped, target in ((False, outs[0]), (True, outs[1])):
        for down in range(3):
            pieces, offsets = [], []
            for along in range(3):
                product = products[(along, down) if flipped else (down, along)]
                pieces += split(product[:pixels], 2)
                offset = jnp.sum(product[pixels : pixels + 3], axis=0, keepdims=True)
                if (down, along) == (1, 1):
                    offset = offset + 0.5 * first_bias
                offsets.append(jnp.concatenate(split(offset, 3), axis=0))
                offsets.append(jnp.zeros((SLOT - 3, width), jnp.float32))
            used = 3 * (2 * pixels + SLOT)
            offsets.append(jnp.zeros((width - used, width), jnp.float32))
            value = jnp.concatenate(pieces + offsets, axis=0)
            target[down * width : (down + 1) * width, :] = value.astype(jnp.bfloat16)
    for load in loads[3:4] + loads[5:]:
        load.wait()
    for ref in (conv_w_kept, conv_b, mix_b):
        ref[...] = (0.5 * ref[...].astype(jnp.float32)).astype(ref.dtype)
    quarter = (0.25 * mix_buf[...].astype(jnp.float32)).astype(jnp.bfloat16)
    mix_w[...] = jnp.concatenate([quarter, quarter], axis=0)
    half = (0.5 * up_buf[...].astype(jnp.float32)).astype(jnp.bfloat16)
    joint = jnp.dot(proj_w[...], half, preferred_element_type=jnp.float32)
    up_w[...] = jnp.concatenate(split(joint, 2), axis=0).astype(jnp.bfloat16)
    pieces = jnp.concatenate(split(proj_b[...].reshape(1, -1), 3), axis=0).astype(jnp.bfloat16)
    shift = jnp.dot(pieces, half, preferred_element_type=jnp.float32)
    up_b[...] = 0.5 * up_b[...] + jnp.sum(shift, axis=0)


def encoder_kernel(
    gathered, first_plain, first_turned, *refs, sizes, shared,
):
    n_row, n_col, tile_rows, tile_cols = sizes
    if shared:
        selects = (None, None)
    else:
        selects, refs = refs[:2], refs[2:]
    conv_w, conv_b, mix_w, mix_b, proj_w, proj_b, up_w, up_b, down_w, down_b = refs[:10]
    latents, sym_out, *buffers = refs[10:]
    _, pixels, cells = gathered.shape
    width = mix_w.shape[1]
    span = n_row * tile_rows
    own_rows = latents.shape[0]
    row = lax.axis_index("row")
    col = lax.axis_index("col")

    def keep_inside(value, start, margin):
        rows = value.shape[0]
        if isinstance(start, int):
            edges = [max(0, min(rows, edge - start)) for edge in (margin, margin + tile_rows)]
        else:
            edges = [rows, rows]
        pieces = []
        for low, high in ((0, edges[0]), (edges[1], rows)):
            first = row * tile_rows - margin + start + low
            lines = [
                jnp.where((first + r >= 0) & (first + r < span), value[low + r], 0.0)[None]
                for r in range(high - low)
            ]
            pieces.append(lines)
        inner = [value[edges[0] : edges[1]]] if edges[1] > edges[0] else []
        return jnp.concatenate(pieces[0] + inner + pieces[1], axis=0)

    def shifted(stage, start, value):
        count = value.shape[0]
        base = 0 if shared else start
        stage[pl.ds(base, count), PAD : PAD + span, :] = value
        return [
            stage[pl.ds(base, count), PAD - 1 + at : PAD - 1 + at + span, :] for at in range(3)
        ]

    def emit(pair, start, value):
        target, stage = pair
        for at, part in enumerate(shifted(stage, start, value)):
            lanes = slice(at * width, (at + 1) * width)
            target[pl.ds(start, value.shape[0]), :, lanes] = part.astype(jnp.bfloat16)

    def patches(pair, flipped):
        target, stage = pair
        group, inner = (n_row, tile_rows) if flipped else (n_col, tile_cols)
        limit = (n_col if flipped else n_row) - 1
        ones = jnp.ones((width - 6 * pixels, cells), jnp.bfloat16)
        columns = [[] for _ in window_tiles(row, flipped, sizes)]
        for column, tile in zip(columns, window_tiles(row, flipped, sizes)):
            at = jnp.clip(tile, 0, limit)
            for g in range(group):
                column.append(gathered[at * n_row + g] if flipped else gathered[g * n_row + at])
        if not flipped:
            lane = lax.broadcasted_iota(jnp.int32, (pixels, cells), 1)
            late = lane >= (tile_rows - LAYERS) * tile_cols
            rims = [
                jnp.where(late, up.astype(jnp.float32), down.astype(jnp.float32))
                for up, down in zip(columns[0], columns[2])
            ]
            columns = [columns[1], [rim.astype(jnp.bfloat16) for rim in rims]]
        columns = [
            jnp.concatenate([part for tile in column for part in [tile] * 6 + [ones]], axis=0)
            for column in columns
        ]
        source = jnp.concatenate(columns, axis=1)

        def step(start, rows):
            if shared:
                select = selection(row, flipped, start, rows, sizes)
            else:
                select = selects[flipped][start * inner : (start + rows) * inner, :]
            value = lax.dot_general(
                select, source, (((1,), (1,)), ((), ())), preferred_element_type=jnp.float32
            )
            value = jnp.concatenate(
                [
                    value[:, g * width : (g + 1) * width].reshape(rows, inner, width)
                    for g in range(group)
                ],
                axis=1,
            )
            before, same, after = shifted(stage, start, value)
            lane = lax.broadcasted_iota(jnp.int32, same.shape, 2)
            which = jnp.where(lane < 6 * pixels, lane // (2 * pixels), (lane - 6 * pixels) // SLOT)
            value = jnp.where(which == 0, before, jnp.where(which == 1, same, after))
            target[pl.ds(start, rows), :, :] = value.astype(jnp.bfloat16)

        return row_steps(tile_rows + 2 * LAYERS, span, step)

    def taps(layer, flipped):
        if layer == 0:
            return (first_turned if flipped else first_plain)[...]
        if flipped:
            blocks = [conv_w[layer - 1, :, a].reshape(3 * width, width) for a in range(3)]
            return jnp.concatenate(blocks, axis=0)
        return conv_w[layer - 1].reshape(9 * width, width)

    def convolve(source, layer, flipped, start, rows, place, extent):
        windows = [
            source[pl.ds(start + a, rows), pl.ds(place, extent), :].reshape(rows * extent, -1)
            for a in range(3)
        ]
        total = jnp.dot(
            jnp.concatenate(windows, axis=1),
            taps(layer, flipped),
            preferred_element_type=jnp.float32,
        )
        if layer > 0:
            total = total + conv_b[layer : layer + 1, :]
        return gelu_of_twice(total).reshape(rows, extent, width)

    def layer_steps(layer, flipped, source, target):
        def step(start, rows):
            value = convolve(source[0], layer, flipped, start, rows, 0, span)
            emit(target, start, keep_inside(value, start, LAYERS - layer - 1))

        return row_steps(tile_rows + 2 * (LAYERS - layer - 1), span, step)

    def last_strip(flipped, source):
        strip = convolve(source[0], LAYERS - 1, flipped, col * own_rows, own_rows, 0, span)
        return strip.astype(jnp.bfloat16)

    def last_tile(flipped, source):
        place = pl.multiple_of(col * tile_cols, tile_cols)
        tile = convolve(source[0], LAYERS - 1, flipped, 0, tile_rows, place, tile_cols)
        return tile.astype(jnp.bfloat16)

    def average(first, second):
        total = first.astype(jnp.float32) + second.astype(jnp.float32)
        return (total * 0.5).astype(jnp.bfloat16)

    half = len(buffers) // 2
    pairs = list(zip(buffers[:half], buffers[half:]))
    for _, stage in pairs:
        stage[:, :PAD, :] = jnp.zeros((stage.shape[0], PAD, width), jnp.float32)
        stage[:, PAD + span :, :] = jnp.zeros((stage.shape[0], PAD, width), jnp.float32)
    plain, turned = pairs[:LAYERS], pairs[-LAYERS:]
    if shared:
        strips, tiles = [], []
        for flipped, chain in ((False, plain), (True, turned)):
            steps = patches(chain[0], flipped)
            for layer in range(LAYERS - 1):
                steps += layer_steps(layer, flipped, chain[layer], chain[layer + 1])
            for thunk in steps:
                thunk()
            strips.append(last_strip(flipped, chain[-1]))
            tiles.append(last_tile(flipped, chain[-1]))
    else:
        in_turn(patches(plain[0], False), patches(turned[0], True))
        in_turn(layer_steps(0, False, plain[0], plain[1]), [])
        in_turn(layer_steps(0, True, turned[0], turned[1]), [])
        in_turn(layer_steps(1, False, plain[1], plain[2]), [])
        in_turn(layer_steps(1, True, turned[1], turned[2]), [])
        strip_m = last_strip(False, plain[-1])
        tile_m = last_tile(False, plain[-1])
        strip_t = last_strip(True, turned[-1])
        tile_t = last_tile(True, turned[-1])
        strips, tiles = [strip_m, strip_t], [tile_m, tile_t]
    sym_out[...] = average(*tiles)
    both = jnp.concatenate([s.reshape(own_rows * span, width) for s in strips], axis=1)
    mixed = jnp.dot(both, mix_w[...], preferred_element_type=jnp.float32) + mix_b[...].reshape(1, width)
    summed = jnp.sum(gelu_of_twice(mixed).reshape(own_rows, span, width), axis=1)
    pooled = (summed / span).astype(jnp.bfloat16)
    latent = jnp.dot(pooled, proj_w[...], preferred_element_type=jnp.float32)
    latent = latent + proj_b[...].reshape(1, -1)
    twice = jnp.concatenate([pooled, pooled], axis=1)
    hidden = jnp.dot(twice, up_w[...], preferred_element_type=jnp.float32)
    hidden = gelu_of_twice(hidden + up_b[...].reshape(1, -1)).astype(jnp.bfloat16)
    result = jnp.dot(hidden, down_w[...], preferred_element_type=jnp.float32)
    latents[...] = (latent + result + down_b[...].reshape(1, -1)).astype(jnp.bfloat16)


def body(contact_map, embed_weight, embed_bias, conv_weight, *rest):
    n_row, n_col = lax.axis_size("row"), lax.axis_size("col")
    tile_rows = contact_map.shape[0] // PATCH
    tile_cols = contact_map.shape[1] // PATCH
    sizes = (n_row, n_col, tile_rows, tile_cols)
    pixels, width = embed_weight.shape
    cells = tile_rows * tile_cols
    span = n_row * tile_rows
    own_rows = tile_rows // n_col
    out_width = rest[-1].shape[0]
    heights = [tile_rows + 2 * (LAYERS - layer) for layer in range(LAYERS)]
    shared = sum(heights) * span > UNROLL_CELLS * 2
    whole = pl.BlockSpec(memory_space=pltpu.VMEM)

    def near(value):
        return pltpu.with_memory_space_constraint(value, pltpu.VMEM)

    shape = (n_row * n_col, pixels, cells)
    sent = pl.pallas_call(
        functools.partial(patch_kernel, tile_rows=tile_rows, tile_cols=tile_cols),
        out_shape=(jax.ShapeDtypeStruct if shared else pltpu.VMEM)(shape, jnp.bfloat16),
        in_specs=[whole],
        out_specs=whole,
        name="patches",
    )(contact_map)
    gathered = lax.all_to_all(sent, ("col", "row"), 0, 0, tiled=True)
    shapes = [(3 * width, width)] * 2
    if not shared:
        turned_tiles = len(window_tiles(0, True, sizes))
        shapes.append((heights[0] * tile_cols, 2 * cells))
        shapes.append((heights[0] * tile_rows, turned_tiles * cells))
    shapes = [pltpu.VMEM(shape, jnp.bfloat16) for shape in shapes]
    matrices = len(shapes) - 2
    later = (LAYERS - 1,) + conv_weight.shape[1:]
    shapes.append(pltpu.VMEM(later, conv_weight.dtype))
    shapes += [pltpu.VMEM(value.shape, value.dtype) for value in rest]
    mix_weight, up_weight = rest[1], rest[5]
    shapes[matrices + 4] = pltpu.VMEM((2 * width, width), jnp.bfloat16)
    shapes[matrices + 8] = pltpu.VMEM((2 * width, up_weight.shape[1]), jnp.bfloat16)
    inputs = (embed_weight, embed_bias, conv_weight, *rest)
    prepared = pl.pallas_call(
        functools.partial(prepare_kernel, sizes=sizes, count=len(inputs), matrices=matrices),
        out_shape=shapes,
        in_specs=[pl.BlockSpec(memory_space=pl.ANY)] * len(inputs),
        out_specs=[whole] * len(shapes),
        scratch_shapes=[
            pltpu.VMEM(embed_weight.shape, embed_weight.dtype),
            pltpu.VMEM(embed_bias.shape, embed_bias.dtype),
            pltpu.VMEM(conv_weight.shape[1:], conv_weight.dtype),
            pltpu.VMEM(mix_weight.shape, mix_weight.dtype),
            pltpu.VMEM(up_weight.shape, up_weight.dtype),
            pltpu.SemaphoreType.DMA((len(inputs) + 1,)),
        ],
        name="prepare",
    )(*inputs)
    prepared = [near(value) for value in prepared]
    operands = [gathered if shared else near(gathered), *prepared]
    in_specs = [whole] * len(operands)
    buffers = [
        pltpu.VMEM((h, span, width * (3 if at else 1)), jnp.bfloat16) for at, h in enumerate(heights)
    ]
    stages = [
        pltpu.VMEM((1 if shared else h, span + 2 * PAD, width), jnp.float32) for h in heights
    ]
    if not shared:
        buffers, stages = buffers * 2, stages * 2
    return pl.pallas_call(
        functools.partial(encoder_kernel, sizes=sizes, shared=shared),
        out_shape=(
            jax.ShapeDtypeStruct((own_rows, out_width), jnp.bfloat16),
            jax.ShapeDtypeStruct((tile_rows, tile_cols, width), jnp.bfloat16),
        ),
        in_specs=in_specs,
        out_specs=(whole, whole),
        scratch_shapes=buffers + stages,
        name="encoder",
    )(*operands)


def solution(mesh):
    return jax.shard_map(
        body,
        mesh=mesh,
        in_specs=(P("row", "col"), P(), P(), P(), P(), P(), P(), P(), P(), P(), P(), P(), P()),
        out_specs=(P(("row", "col"), None), P("row", "col", None)),
        check_vma=False,
    )
```

```python
import functools
import itertools

import jax
import jax.numpy as jnp
from jax import lax
from jax.experimental import pallas as pl
from jax.experimental.pallas import tpu as pltpu
from jax.sharding import PartitionSpec as P

PATCH = 4
LAYERS = 3
UNROLL_CELLS = 2048
CHUNK_CELLS = 1024
PAD = 8
PIECE = 32
SLOT = 8


def gelu_of_twice(half):
    scale = 2 * 0.7978845608028654
    return half + half * jnp.tanh(half * (scale + (4 * scale * 0.044715) * (half * half)))


def row_steps(total, span, step):
    if total * span <= UNROLL_CELLS:
        chunk = max(1, CHUNK_CELLS // span)
        starts = range(0, total, chunk)
        return [functools.partial(step, s, min(chunk, total - s)) for s in starts]
    return [lambda: lax.fori_loop(0, total, lambda r, carry: (step(r, 1), carry)[1], 0)]


def in_turn(first, second):
    for mine, other in itertools.zip_longest(first, second):
        for thunk in (mine, other):
            if thunk is not None:
                thunk()


def window_tiles(row, flipped, sizes):
    n_row, n_col, tile_rows, tile_cols = sizes
    if not flipped:
        return [row - 1, row, row + 1]
    first = (row * tile_rows - LAYERS + tile_cols) // tile_cols - 1
    starts = [r * tile_rows - LAYERS for r in range(n_row)]
    reach = tile_rows + 2 * LAYERS - 1
    count = max((f + reach) // tile_cols - f // tile_cols + 1 for f in starts)
    return [first + t for t in range(count)]


def selection(row, flipped, start, rows, sizes):
    n_row, n_col, tile_rows, tile_cols = sizes
    inner, outer, limit = (tile_rows, tile_cols, n_col) if flipped else (tile_cols, tile_rows, n_row)
    cells = tile_rows * tile_cols
    shape = (rows, inner, cells)
    major = lax.broadcasted_iota(jnp.int32, shape, 0) + (start + row * tile_rows - LAYERS)
    minor = lax.broadcasted_iota(jnp.int32, shape, 1)
    lane = lax.broadcasted_iota(jnp.int32, shape, 2)
    blocks = []
    for tile in window_tiles(row, flipped, sizes):
        offset = major - tile * outer
        goal = minor * tile_cols + offset if flipped else offset * tile_cols + minor
        ok = (offset >= 0) & (offset < outer) & (major >= 0) & (major < limit * outer)
        block = jnp.where(ok & (lane == goal), 1.0, 0.0)
        blocks.append(block.reshape(rows * inner, cells))
    if not flipped:
        blocks = [blocks[1], blocks[0] + blocks[2]]
    return jnp.concatenate([block.astype(jnp.bfloat16) for block in blocks], axis=1)


def split(value, count):
    parts = []
    for _ in range(count):
        part = value.astype(jnp.bfloat16).astype(jnp.float32)
        parts.append(part)
        value = value - part
    return parts


def patch_kernel(tile, sent, *, tile_rows, tile_cols):
    height, span = tile.shape
    cells = tile_rows * tile_cols
    shape = (span, PATCH * cells)
    pixel = lax.broadcasted_iota(jnp.int32, shape, 0)
    lane = lax.broadcasted_iota(jnp.int32, shape, 1)
    goal = (lane % tile_cols) * PATCH + lane // cells
    spread = jnp.where(pixel == goal, 1.0, 0.0).astype(jnp.bfloat16)
    wide = jnp.dot(tile[...].astype(jnp.bfloat16), spread, preferred_element_type=jnp.float32)
    line = lax.broadcasted_iota(jnp.int32, wide.shape, 0) // PATCH
    lane = lax.broadcasted_iota(jnp.int32, wide.shape, 1)
    wide = jnp.where(line == (lane % cells) // tile_cols, wide, 0.0)
    pair = 2 * PATCH
    summed = sum(wide[at : at + pair] for at in range(pair, height, pair)) + wide[:pair]
    summed = summed[:PATCH] + summed[PATCH:]
    blocks = [summed[:, b * cells : (b + 1) * cells] for b in range(PATCH)]
    result = jnp.concatenate(blocks, axis=0).astype(jnp.bfloat16)
    sent[...] = jnp.broadcast_to(result[None], sent.shape)


def prepare_kernel(*refs, sizes, count, matrices):
    embed_w, embed_b, conv_w, *others = refs[:count]
    outs = refs[count : count + 2 + matrices]
    kept = refs[count + 2 + matrices : -6]
    conv_w_kept, conv_b, mix_w, mix_b, proj_w, proj_b, up_w, up_b, _, _ = kept
    embed_buf, bias_buf, conv_buf, mix_buf, up_buf, arrived = refs[-6:]
    sources = [embed_w, embed_b, conv_w.at[0], conv_w.at[pl.ds(1, LAYERS - 1)], *others]
    targets = [embed_buf, bias_buf, conv_buf, *kept]
    targets[5], targets[9] = mix_buf, up_buf
    loads = [
        pltpu.make_async_copy(source, target, arrived.at[at])
        for at, (source, target) in enumerate(zip(sources, targets))
    ]
    for load in loads:
        load.start()
    if matrices:
        row = lax.axis_index("row")
        for flipped, target in ((False, outs[2]), (True, outs[3])):
            target[...] = selection(row, flipped, 0, sizes[2] + 2 * LAYERS, sizes)
    for load in loads[:3] + loads[4:5]:
        load.wait()
    embed_w, embed_b = embed_buf, bias_buf
    first_bias = conv_b[0:1, :]
    pixels, width = embed_w.shape
    bias = jnp.concatenate(split(embed_b[...].reshape(1, width), 3), axis=0)
    rest = jnp.zeros((PIECE - pixels - 3, width), jnp.float32)
    lines = embed_w[...].astype(jnp.float32)
    order = [PATCH * a + b for b in range(PATCH) for a in range(PATCH)]
    left = jnp.concatenate([lines[p : p + 1] for p in order] + [bias, rest], axis=0)
    left = (0.5 * left).astype(jnp.bfloat16)
    products = {}
    for a, b in itertools.product(range(3), range(3)):
        products[a, b] = jnp.dot(left, conv_buf[a, b], preferred_element_type=jnp.float32)
    for flipped, target in ((False, outs[0]), (True, outs[1])):
        for down in range(3):
            pieces, offsets = [], []
            for along in range(3):
                product = products[(along, down) if flipped else (down, along)]
                pieces += split(product[:pixels], 2)
                offset = jnp.sum(product[pixels : pixels + 3], axis=0, keepdims=True)
                if (down, along) == (1, 1):
                    offset = offset + 0.5 * first_bias
                offsets.append(jnp.concatenate(split(offset, 3), axis=0))
                offsets.append(jnp.zeros((SLOT - 3, width), jnp.float32))
            used = 3 * (2 * pixels + SLOT)
            offsets.append(jnp.zeros((width - used, width), jnp.float32))
            value = jnp.concatenate(pieces + offsets, axis=0)
            target[down * width : (down + 1) * width, :] = value.astype(jnp.bfloat16)
    for load in loads[3:4] + loads[5:]:
        load.wait()
    for ref in (conv_w_kept, conv_b, mix_b):
        ref[...] = (0.5 * ref[...].astype(jnp.float32)).astype(ref.dtype)
    quarter = (0.25 * mix_buf[...].astype(jnp.float32)).astype(jnp.bfloat16)
    mix_w[...] = jnp.concatenate([quarter, quarter], axis=0)
    half = (0.5 * up_buf[...].astype(jnp.float32)).astype(jnp.bfloat16)
    joint = jnp.dot(proj_w[...], half, preferred_element_type=jnp.float32)
    up_w[...] = jnp.concatenate(split(joint, 2), axis=0).astype(jnp.bfloat16)
    pieces = jnp.concatenate(split(proj_b[...].reshape(1, -1), 3), axis=0).astype(jnp.bfloat16)
    shift = jnp.dot(pieces, half, preferred_element_type=jnp.float32)
    up_b[...] = 0.5 * up_b[...] + jnp.sum(shift, axis=0)


def encoder_kernel(
    gathered, first_plain, first_turned, *refs, sizes, shared,
):
    n_row, n_col, tile_rows, tile_cols = sizes
    if shared:
        selects = (None, None)
    else:
        selects, refs = refs[:2], refs[2:]
    conv_w, conv_b, mix_w, mix_b, proj_w, proj_b, up_w, up_b, down_w, down_b = refs[:10]
    latents, sym_out, *buffers = refs[10:]
    _, pixels, cells = gathered.shape
    width = mix_w.shape[1]
    span = n_row * tile_rows
    own_rows = latents.shape[0]
    row = lax.axis_index("row")
    col = lax.axis_index("col")

    def keep_inside(value, start, margin):
        rows = value.shape[0]
        if isinstance(start, int):
            edges = [max(0, min(rows, edge - start)) for edge in (margin, margin + tile_rows)]
        else:
            edges = [rows, rows]
        pieces = []
        for low, high in ((0, edges[0]), (edges[1], rows)):
            first = row * tile_rows - margin + start + low
            lines = [
                jnp.where((first + r >= 0) & (first + r < span), value[low + r], 0.0)[None]
                for r in range(high - low)
            ]
            pieces.append(lines)
        inner = [value[edges[0] : edges[1]]] if edges[1] > edges[0] else []
        return jnp.concatenate(pieces[0] + inner + pieces[1], axis=0)

    def shifted(stage, start, value):
        count = value.shape[0]
        base = 0 if shared else start
        stage[pl.ds(base, count), PAD : PAD + span, :] = value
        before, after = [
            stage[pl.ds(base, count), PAD + at : PAD + at + span, :] for at in (-1, 1)
        ]
        return [before, value, after]

    def emit(pair, start, value):
        target, stage = pair
        for at, part in enumerate(shifted(stage, start, value)):
            lanes = slice(at * width, (at + 1) * width)
            target[pl.ds(start, value.shape[0]), :, lanes] = part.astype(jnp.bfloat16)

    def patches(pair, flipped):
        target, stage = pair
        group, inner = (n_row, tile_rows) if flipped else (n_col, tile_cols)
        limit = (n_col if flipped else n_row) - 1
        ones = jnp.ones((width - 6 * pixels, cells), jnp.bfloat16)
        columns = [[] for _ in window_tiles(row, flipped, sizes)]
        for column, tile in zip(columns, window_tiles(row, flipped, sizes)):
            at = jnp.clip(tile, 0, limit)
            for g in range(group):
                column.append(gathered[at * n_row + g] if flipped else gathered[g * n_row + at])
        if not flipped:
            lane = lax.broadcasted_iota(jnp.int32, (pixels, cells), 1)
            late = lane >= (tile_rows - LAYERS) * tile_cols
            rims = [
                jnp.where(late, up.astype(jnp.float32), down.astype(jnp.float32))
                for up, down in zip(columns[0], columns[2])
            ]
            columns = [columns[1], [rim.astype(jnp.bfloat16) for rim in rims]]
        columns = [
            jnp.concatenate([part for tile in column for part in [tile] * 6 + [ones]], axis=0)
            for column in columns
        ]
        source = jnp.concatenate(columns, axis=1)

        def step(start, rows):
            if shared:
                select = selection(row, flipped, start, rows, sizes)
            else:
                select = selects[flipped][start * inner : (start + rows) * inner, :]
            value = lax.dot_general(
                select, source, (((1,), (1,)), ((), ())), preferred_element_type=jnp.float32
            )
            value = jnp.concatenate(
                [
                    value[:, g * width : (g + 1) * width].reshape(rows, inner, width)
                    for g in range(group)
                ],
                axis=1,
            )
            before, same, after = shifted(stage, start, value)
            lane = lax.broadcasted_iota(jnp.int32, same.shape, 2)
            which = jnp.where(lane < 6 * pixels, lane // (2 * pixels), (lane - 6 * pixels) // SLOT)
            value = jnp.where(which == 0, before, jnp.where(which == 1, same, after))
            target[pl.ds(start, rows), :, :] = value.astype(jnp.bfloat16)

        return row_steps(tile_rows + 2 * LAYERS, span, step)

    def taps(layer, flipped):
        if layer == 0:
            return (first_turned if flipped else first_plain)[...]
        if flipped:
            blocks = [conv_w[layer - 1, :, a].reshape(3 * width, width) for a in range(3)]
            return jnp.concatenate(blocks, axis=0)
        return conv_w[layer - 1].reshape(9 * width, width)

    def convolve(source, layer, flipped, start, rows, place, extent):
        windows = [
            source[pl.ds(start + a, rows), pl.ds(place, extent), :].reshape(rows * extent, -1)
            for a in range(3)
        ]
        total = jnp.dot(
            jnp.concatenate(windows, axis=1),
            taps(layer, flipped),
            preferred_element_type=jnp.float32,
        )
        if layer > 0:
            total = total + conv_b[layer : layer + 1, :]
        return gelu_of_twice(total).reshape(rows, extent, width)

    def layer_steps(layer, flipped, source, target):
        def step(start, rows):
            value = convolve(source[0], layer, flipped, start, rows, 0, span)
            emit(target, start, keep_inside(value, start, LAYERS - layer - 1))

        return row_steps(tile_rows + 2 * (LAYERS - layer - 1), span, step)

    def last_strip(flipped, source):
        strip = convolve(source[0], LAYERS - 1, flipped, col * own_rows, own_rows, 0, span)
        return strip.astype(jnp.bfloat16)

    def last_tile(flipped, source):
        place = pl.multiple_of(col * tile_cols, tile_cols)
        tile = convolve(source[0], LAYERS - 1, flipped, 0, tile_rows, place, tile_cols)
        return tile.astype(jnp.bfloat16)

    def average(first, second):
        total = first.astype(jnp.float32) + second.astype(jnp.float32)
        return (total * 0.5).astype(jnp.bfloat16)

    half = len(buffers) // 2
    pairs = list(zip(buffers[:half], buffers[half:]))
    for _, stage in pairs:
        stage[:, :PAD, :] = jnp.zeros((stage.shape[0], PAD, width), jnp.float32)
        stage[:, PAD + span :, :] = jnp.zeros((stage.shape[0], PAD, width), jnp.float32)
    plain, turned = pairs[:LAYERS], pairs[-LAYERS:]
    if shared:
        strips, tiles = [], []
        for flipped, chain in ((False, plain), (True, turned)):
            steps = patches(chain[0], flipped)
            for layer in range(LAYERS - 1):
                steps += layer_steps(layer, flipped, chain[layer], chain[layer + 1])
            for thunk in steps:
                thunk()
            strips.append(last_strip(flipped, chain[-1]))
            tiles.append(last_tile(flipped, chain[-1]))
    else:
        in_turn(patches(plain[0], False), patches(turned[0], True))
        in_turn(layer_steps(0, False, plain[0], plain[1]), [])
        in_turn(layer_steps(0, True, turned[0], turned[1]), [])
        in_turn(layer_steps(1, False, plain[1], plain[2]), [])
        in_turn(layer_steps(1, True, turned[1], turned[2]), [])
        strip_m = last_strip(False, plain[-1])
        tile_m = last_tile(False, plain[-1])
        strip_t = last_strip(True, turned[-1])
        tile_t = last_tile(True, turned[-1])
        strips, tiles = [strip_m, strip_t], [tile_m, tile_t]
    sym_out[...] = average(*tiles)
    both = jnp.concatenate([s.reshape(own_rows * span, width) for s in strips], axis=1)
    mixed = jnp.dot(both, mix_w[...], preferred_element_type=jnp.float32) + mix_b[...].reshape(1, width)
    summed = jnp.sum(gelu_of_twice(mixed).reshape(own_rows, span, width), axis=1)
    pooled = (summed / span).astype(jnp.bfloat16)
    latent = jnp.dot(pooled, proj_w[...], preferred_element_type=jnp.float32)
    latent = latent + proj_b[...].reshape(1, -1)
    twice = jnp.concatenate([pooled, pooled], axis=1)
    hidden = jnp.dot(twice, up_w[...], preferred_element_type=jnp.float32)
    hidden = gelu_of_twice(hidden + up_b[...].reshape(1, -1)).astype(jnp.bfloat16)
    result = jnp.dot(hidden, down_w[...], preferred_element_type=jnp.float32)
    latents[...] = (latent + result + down_b[...].reshape(1, -1)).astype(jnp.bfloat16)


def body(contact_map, embed_weight, embed_bias, conv_weight, *rest):
    n_row, n_col = lax.axis_size("row"), lax.axis_size("col")
    tile_rows = contact_map.shape[0] // PATCH
    tile_cols = contact_map.shape[1] // PATCH
    sizes = (n_row, n_col, tile_rows, tile_cols)
    pixels, width = embed_weight.shape
    cells = tile_rows * tile_cols
    span = n_row * tile_rows
    own_rows = tile_rows // n_col
    out_width = rest[-1].shape[0]
    heights = [tile_rows + 2 * (LAYERS - layer) for layer in range(LAYERS)]
    shared = sum(heights) * span > UNROLL_CELLS * 2
    whole = pl.BlockSpec(memory_space=pltpu.VMEM)

    def near(value):
        return pltpu.with_memory_space_constraint(value, pltpu.VMEM)

    shape = (n_row * n_col, pixels, cells)
    sent = pl.pallas_call(
        functools.partial(patch_kernel, tile_rows=tile_rows, tile_cols=tile_cols),
        out_shape=(jax.ShapeDtypeStruct if shared else pltpu.VMEM)(shape, jnp.bfloat16),
        in_specs=[whole],
        out_specs=whole,
        name="patches",
    )(contact_map)
    gathered = lax.all_to_all(sent, ("col", "row"), 0, 0, tiled=True)
    shapes = [(3 * width, width)] * 2
    if not shared:
        turned_tiles = len(window_tiles(0, True, sizes))
        shapes.append((heights[0] * tile_cols, 2 * cells))
        shapes.append((heights[0] * tile_rows, turned_tiles * cells))
    shapes = [pltpu.VMEM(shape, jnp.bfloat16) for shape in shapes]
    matrices = len(shapes) - 2
    later = (LAYERS - 1,) + conv_weight.shape[1:]
    shapes.append(pltpu.VMEM(later, conv_weight.dtype))
    shapes += [pltpu.VMEM(value.shape, value.dtype) for value in rest]
    mix_weight, up_weight = rest[1], rest[5]
    shapes[matrices + 4] = pltpu.VMEM((2 * width, width), jnp.bfloat16)
    shapes[matrices + 8] = pltpu.VMEM((2 * width, up_weight.shape[1]), jnp.bfloat16)
    inputs = (embed_weight, embed_bias, conv_weight, *rest)
    prepared = pl.pallas_call(
        functools.partial(prepare_kernel, sizes=sizes, count=len(inputs), matrices=matrices),
        out_shape=shapes,
        in_specs=[pl.BlockSpec(memory_space=pl.ANY)] * len(inputs),
        out_specs=[whole] * len(shapes),
        scratch_shapes=[
            pltpu.VMEM(embed_weight.shape, embed_weight.dtype),
            pltpu.VMEM(embed_bias.shape, embed_bias.dtype),
            pltpu.VMEM(conv_weight.shape[1:], conv_weight.dtype),
            pltpu.VMEM(mix_weight.shape, mix_weight.dtype),
            pltpu.VMEM(up_weight.shape, up_weight.dtype),
            pltpu.SemaphoreType.DMA((len(inputs) + 1,)),
        ],
        name="prepare",
    )(*inputs)
    prepared = [near(value) for value in prepared]
    operands = [gathered if shared else near(gathered), *prepared]
    in_specs = [whole] * len(operands)
    buffers = [
        pltpu.VMEM((h, span, width * (3 if at else 1)), jnp.bfloat16) for at, h in enumerate(heights)
    ]
    stages = [
        pltpu.VMEM((1 if shared else h, span + 2 * PAD, width), jnp.float32) for h in heights
    ]
    if not shared:
        buffers, stages = buffers * 2, stages * 2
    return pl.pallas_call(
        functools.partial(encoder_kernel, sizes=sizes, shared=shared),
        out_shape=(
            jax.ShapeDtypeStruct((own_rows, out_width), jnp.bfloat16),
            jax.ShapeDtypeStruct((tile_rows, tile_cols, width), jnp.bfloat16),
        ),
        in_specs=in_specs,
        out_specs=(whole, whole),
        scratch_shapes=buffers + stages,
        name="encoder",
    )(*operands)


def solution(mesh):
    return jax.shard_map(
        body,
        mesh=mesh,
        in_specs=(P("row", "col"), P(), P(), P(), P(), P(), P(), P(), P(), P(), P(), P(), P()),
        out_specs=(P(("row", "col"), None), P("row", "col", None)),
        check_vma=False,
    )
```
